32 devices in a mesh: groups: 2 (over y), seq: 4 (over z), heads: 2 (over x), cfg: 2 (over core).
Axes of the slice: x: 2, y: 2, z: 4, core: 2. Of those that a mesh axis runs over, the one named last changes fastest.
Arguments:
- video_tokens: bfloat16 [2, 8, 1152, 1024], P('cfg', ('groups', 'seq'), 'heads'), parts along dimension 1, may hold values from -6 to 6
- text_tokens: bfloat16 [2, 8, 1152, 128], P('cfg', ('groups', 'seq'), 'heads'), parts along dimension 1, may hold values from -6 to 6
- text_length: int32 [2, 8], P('cfg', ('groups', 'seq')), parts along dimension 1, may hold values from 1 to 128
- guide_numer: int32 [8], P(('groups', 'seq')), parts along dimension 0, may hold values from 2 to 8
- guide_denom: int32 [8], P(('groups', 'seq')), parts along dimension 0, may hold values from 4 to 8
- spatial_gain: bfloat16 [1152], replicated, may hold values from 0.25 to 1.75
- spatial_qkv: bfloat16 [3, 1152, 1152], P(None, 'heads'), may hold values from -0.11785113 to 0.11785113
- spatial_out: bfloat16 [1152, 1152], P('heads'), may hold values from -0.1875 to 0.1875
- temporal_gain: bfloat16 [1152], replicated, may hold values from 0.25 to 1.75
- temporal_qkv: bfloat16 [3, 1152, 1152], P(None, 'heads'), may hold values from -0.11785113 to 0.11785113
- temporal_out: bfloat16 [1152, 1152], P('heads'), may hold values from -0.1875 to 0.1875
Outputs:
- guided: bfloat16 [8, 1152, 1024], P(('groups', 'seq'), ('heads', 'cfg')), parts along dimension 0
The draws below stay inside these ranges and needn't reach their ends.
There are 2 independent parts, one for each index of `groups`. The reference program is written for one: setup_inputs(seed, part) draws one part's arguments, and reference() takes and returns one part's arrays. A program takes and returns all parts, laid end to end along the dimension named above; an argument that names none is the same for every part. Nothing has to cross between parts.
Inputs may be any that keep to these rules, and one draw needn't show every extreme that they name: `text_length`: text tokens at or beyond a frame's length are padding.
All inputs are finite; a program needn't handle non-finite values.
Results may differ from the reference program's by a relative error of at most 0.009.
Values may be sent and summed in bfloat16 or wider, within the bound.
No kernel may reach another device: no remote copies, remote signals or barrier semaphores. Data moves between devices by JAX's collectives and lax.ppermute only.
A program may use at most 64 MiB of HBM per device.

```python
import jax
import jax.numpy as jnp
from jax import lax

D = 1152
HEADS = 16
HEAD_DIM = 72
POS = 1024
TXT = 128
FRAMES = 4


def projection_law(key):
    sigma = D ** (-0.5)
    first = jax.random.fold_in(key, 0)
    values = jnp.clip(jax.random.normal(first, (3, D, D), jnp.float32), -4.0, 4.0) * sigma
    return values.astype(jnp.bfloat16)


def draw_spatial_qkv(key, part):
    return projection_law(jax.random.fold_in(key, 11))


def draw_temporal_qkv(key, part):
    return projection_law(jax.random.fold_in(key, 23))


def draw_video_tokens(key, part):
    key = jax.random.fold_in(key, 31)
    first = jax.random.fold_in(key, 0)
    shape = (2, FRAMES, D, POS)
    values = jnp.clip(jax.random.normal(first, shape, jnp.float32), -6.0, 6.0)
    return values.astype(jnp.bfloat16)


def touch_ends(entries, own_key, low, top_value):
    longest = entries.shape.index(max(entries.shape))
    spots = []
    for shift in (0, 1):
        where = [jax.random.randint(jax.random.fold_in(own_key, axis), (), 0, length) for axis, length in enumerate(entries.shape)]
        where[longest] = (where[longest] + shift) % entries.shape[longest]
        spots.append(tuple(where))
    return entries.at[spots[0]].set(low).at[spots[1]].set(top_value)


def level_of(stream_key, shape, cuts, least, largest):
    level, own = 1.0, jax.random.fold_in(stream_key, 6)
    for position, shards_of in cuts:
        steps = jnp.exp(jax.random.uniform(jax.random.fold_in(own, position), (shards_of,), jnp.float32, least / len(cuts), largest / len(cuts)))
        level = level * jnp.repeat(steps, shape[position] // shards_of).reshape([-1 if axis == position else 1 for axis in range(len(shape))])
    return level


def normal_values(stream_key, shape, scale, most, pieces=(), kind=jnp.bfloat16):
    drawn = jax.random.normal(stream_key, shape, jnp.float32) * scale
    if len(pieces) > 0:
        drawn = level_of(stream_key, shape, pieces, -0.22, 0.18) * drawn
    return jnp.clip(drawn, min=-most, max=most).astype(kind)


def setup_inputs(seed: int = 0, part: int = 0) -> dict:
    key_list = jax.random.split(jax.random.key(seed), 12)
    own_keys = jax.random.split(jax.random.fold_in(key_list[11], part), 12)
    video_tokens = draw_video_tokens(jax.random.fold_in(jax.random.fold_in(key_list[11], part), 71), part)
    text_tokens = normal_values(own_keys[1], (2, FRAMES, D, TXT), 1.0, 6.0, ((0, 2), (1, 4), (2, 2)))
    text_length = touch_ends(jax.random.randint(own_keys[2], (2, FRAMES), 1, TXT + 1), jax.random.fold_in(own_keys[2], 1), 1, TXT).astype(jnp.int32)
    guide_numer = touch_ends(jax.random.randint(own_keys[3], (FRAMES,), 2, 9), jax.random.fold_in(own_keys[3], 1), 2, 8).astype(jnp.int32)
    guide_denom = touch_ends(jax.random.randint(own_keys[4], (FRAMES,), 4, 9), jax.random.fold_in(own_keys[4], 1), 4, 8).astype(jnp.int32)
    spatial_gain = jnp.clip(1.0 + 0.15 * jax.random.normal(key_list[5], (D,), jnp.float32), 0.25, 1.75).astype(jnp.bfloat16)
    spatial_qkv = draw_spatial_qkv(jax.random.fold_in(key_list[11], 71), part)
    spatial_out = normal_values(key_list[7], (D, D), D ** -0.5, 0.1875, ((0, 2),))
    temporal_gain = jnp.clip(1.0 + 0.15 * jax.random.normal(key_list[8], (D,), jnp.float32), 0.25, 1.75).astype(jnp.bfloat16)
    temporal_qkv = draw_temporal_qkv(jax.random.fold_in(key_list[11], 71), part)
    temporal_out = normal_values(key_list[10], (D, D), D ** -0.5, 0.1875, ((0, 2),))
    return dict(video_tokens=video_tokens, text_tokens=text_tokens, text_length=text_length, guide_numer=guide_numer, guide_denom=guide_denom, spatial_gain=spatial_gain, spatial_qkv=spatial_qkv, spatial_out=spatial_out, temporal_gain=temporal_gain, temporal_qkv=temporal_qkv, temporal_out=temporal_out)


epsilon = 1e-06

def normed_project(token_rows, gain_vector, weight_matrix):
    values_wide = token_rows.astype(jnp.float32)
    inverse = lax.rsqrt(lax.optimization_barrier(jnp.mean(values_wide * values_wide, axis=-1)) + epsilon)
    scaled = (values_wide * gain_vector.astype(jnp.float32)).astype(jnp.bfloat16)
    product = jnp.dot(scaled, weight_matrix, preferred_element_type=jnp.float32)
    return (product * inverse[:, None]).astype(jnp.bfloat16)

def softmax_rows(scores):
    top_score = lax.optimization_barrier(jnp.max(scores, axis=-1, keepdims=True))
    expons = jnp.exp(scores - top_score)
    return (expons / lax.optimization_barrier(jnp.sum(expons, axis=-1, keepdims=True))).astype(jnp.bfloat16)

def spatial_attend(query_rows, key_rows, value_rows, valid_keys):
    scores = jnp.einsum('qhe,khe->hqk', query_rows.astype(jnp.float32), key_rows.astype(jnp.float32))
    scores = scores * HEAD_DIM ** (-0.5)
    scores = jnp.where(valid_keys[None, None, :], scores, -jnp.inf)
    weights = softmax_rows(scores)
    result = jnp.einsum('hqk,khe->qhe', weights.astype(jnp.float32), value_rows.astype(jnp.float32))
    return result.astype(jnp.bfloat16)

def reference(video_tokens, text_tokens, text_length, guide_numer, guide_denom, spatial_gain, spatial_qkv, spatial_out, temporal_gain, temporal_qkv, temporal_out):
    frames_all = video_tokens.shape[1]
    spatial_cols = jnp.transpose(spatial_qkv, (2, 0, 1)).reshape(D, 3 * D)
    temporal_cols = jnp.transpose(temporal_qkv, (2, 0, 1)).reshape(D, 3 * D)
    spatial_right = jnp.transpose(spatial_out)
    temporal_right = jnp.transpose(temporal_out)
    outputs = []
    for branch in range(2):
        video_rows = jnp.swapaxes(video_tokens[branch], 1, 2)
        text_rows = jnp.swapaxes(text_tokens[branch], 1, 2)

        def frame_step(inputs):
            frame_rows, frame_text, live_count = inputs
            mixed = normed_project(frame_rows, spatial_gain, spatial_cols).reshape(POS, 3, HEADS, HEAD_DIM)
            context = normed_project(frame_text, spatial_gain, spatial_cols).reshape(TXT, 3, HEADS, HEAD_DIM)
            key_rows = jnp.concatenate([mixed[:, 1], context[:, 1]], axis=0)
            value_rows = jnp.concatenate([mixed[:, 2], context[:, 2]], axis=0)
            valid_keys = jnp.concatenate([jnp.ones((POS,), dtype=bool), jnp.arange(TXT, dtype=jnp.int32) < live_count])
            attended = spatial_attend(mixed[:, 0], key_rows, value_rows, valid_keys).reshape(POS, D)
            update = jnp.dot(attended, spatial_right, preferred_element_type=jnp.float32)
            return (frame_rows.astype(jnp.float32) + update).astype(jnp.bfloat16)
        after_spatial = lax.map(frame_step, (video_rows, text_rows, text_length[branch]))
        flat_rows = after_spatial.reshape(frames_all * POS, D)
        mixed_time = normed_project(flat_rows, temporal_gain, temporal_cols).reshape(frames_all, POS, 3, HEADS, HEAD_DIM)
        scores = jnp.einsum('fphe,gphe->phfg', mixed_time[:, :, 0].astype(jnp.float32), mixed_time[:, :, 1].astype(jnp.float32))
        weights = softmax_rows(scores * HEAD_DIM ** (-0.5))
        attended_time = jnp.einsum('phfg,gphe->fphe', weights.astype(jnp.float32), mixed_time[:, :, 2].astype(jnp.float32))
        attended_time = attended_time.astype(jnp.bfloat16).reshape(frames_all * POS, D)
        update_time = jnp.dot(attended_time, temporal_right, preferred_element_type=jnp.float32)
        block_out = (flat_rows.astype(jnp.float32) + update_time).astype(jnp.bfloat16)
        outputs.append(block_out.reshape(frames_all, POS, D).astype(jnp.float32))
    ratio = guide_numer.astype(jnp.float32) / guide_denom.astype(jnp.float32)
    cond_out = outputs[0]
    uncond_out = outputs[1]
    guided_rows = (uncond_out + ratio[:, None, None] * (cond_out - uncond_out)).astype(jnp.bfloat16)
    return jnp.swapaxes(guided_rows, 1, 2)
```

```python
import functools

import jax
import jax.numpy as jnp
from jax import lax
from jax.experimental import pallas as pl
from jax.experimental.pallas import tpu as pltpu
from jax.sharding import PartitionSpec as P

D = 1152
HEAD_DIM = 72
HEAD_ROWS = 80
LANES = 128
VMEM_LIMIT = 56 * 1024 * 1024


epsilon = 1e-06


def from_partner(shard, axis, stride):
    return lax.ppermute(shard, axis, [(i, i ^ 1 << stride) for i in range(lax.axis_size(axis))])


def softmax_along(scores, axis):
    top_score = jnp.max(scores, axis=axis, keepdims=True)
    expons = jnp.exp(scores - top_score)
    return (expons / jnp.sum(expons, axis=axis, keepdims=True)).astype(jnp.bfloat16)


def project_piece(piece, gain_vector, weights, parts):
    gain_piece = gain_vector.astype(jnp.float32)
    weight_piece = weights[parts]
    piece_wide = piece.astype(jnp.float32)
    scaled = (piece_wide * gain_piece[None, :, None]).astype(jnp.bfloat16)
    product = jnp.einsum("kod,fdp->fkop", weight_piece, scaled, preferred_element_type=jnp.float32)
    return (product, jnp.sum(piece_wide * piece_wide, axis=1))


def add_mixed(piece, matrix):
    return jnp.einsum("oc,fcp->fop", matrix, piece, preferred_element_type=jnp.float32)


def shards_plain(
    video_tokens,
    text_tokens,
    text_length,
    guide_numer,
    guide_denom,
    spatial_gain,
    spatial_qkv,
    spatial_out,
    temporal_gain,
    temporal_qkv,
    temporal_out,
):
    frame_count = video_tokens.shape[1]
    width = video_tokens.shape[2]
    positions = video_tokens.shape[3]
    text_count = text_tokens.shape[3]
    local_heads = width // HEAD_DIM
    frame_tokens = video_tokens[0]
    frame_text = text_tokens[0]
    video_piece = lax.all_gather(frame_tokens, "heads", axis=1, tiled=True)
    text_piece = lax.all_gather(frame_text, "heads", axis=1, tiled=True)
    video_add, video_sq = project_piece(video_piece, spatial_gain, spatial_qkv, slice(0, 3))
    text_add, text_sq = project_piece(text_piece, spatial_gain, spatial_qkv, slice(1, 3))
    mixed = (video_add * lax.rsqrt(video_sq / D + epsilon)[:, None, None, :]).astype(jnp.bfloat16)
    mixed = mixed.reshape(frame_count, 3, local_heads, HEAD_DIM, positions)
    context = (text_add * lax.rsqrt(text_sq / D + epsilon)[:, None, None, :]).astype(jnp.bfloat16)
    context = context.reshape(frame_count, 2, local_heads, HEAD_DIM, text_count)
    key_rows = jnp.concatenate([mixed[:, 1], context[:, 0]], axis=3)
    value_rows = jnp.concatenate([mixed[:, 2], context[:, 1]], axis=3)
    query_all = mixed[:, 0]
    text_valid = jnp.arange(text_count, dtype=jnp.int32)[None, :] < text_length[0][:, None]
    valid_keys = jnp.concatenate(
        [jnp.ones((frame_count, positions), dtype=bool), text_valid], axis=1
    )
    block_rows = min(512, positions)
    block_count = positions // block_rows
    frame_ids = jnp.repeat(jnp.arange(frame_count, dtype=jnp.int32), block_count)
    block_ids = jnp.tile(jnp.arange(block_count, dtype=jnp.int32), frame_count)

    def block_step(inputs):
        frame_id, block_id = inputs
        query_rows = lax.dynamic_slice_in_dim(
            query_all[frame_id], block_id * block_rows, block_rows, 2
        )
        scores = jnp.einsum(
            "hep,hek->hpk", query_rows, key_rows[frame_id], preferred_element_type=jnp.float32
        )
        scores = scores * HEAD_DIM ** (-0.5)
        scores = jnp.where(valid_keys[frame_id][None, None, :], scores, -jnp.inf)
        weights = softmax_along(scores, 2)
        result = jnp.einsum(
            "hpk,hek->hep", weights, value_rows[frame_id], preferred_element_type=jnp.float32
        )
        return result.astype(jnp.bfloat16)

    attended = lax.map(block_step, (frame_ids, block_ids))
    attended = attended.reshape(frame_count, block_count, local_heads, HEAD_DIM, block_rows)
    attended = jnp.transpose(attended, (0, 2, 3, 1, 4)).reshape(frame_count, width, positions)
    update = add_mixed(lax.all_gather(attended, "heads", axis=1, tiled=True), spatial_out)
    after_spatial = (frame_tokens.astype(jnp.float32) + update).astype(jnp.bfloat16)
    own_rows = lax.all_to_all(after_spatial, "seq", split_axis=2, concat_axis=0, tiled=True)
    frames_all = own_rows.shape[0]
    columns = own_rows.shape[2]
    piece_add, piece_sq = project_piece(
        lax.all_gather(own_rows, "heads", axis=1, tiled=True),
        temporal_gain,
        temporal_qkv,
        slice(0, 3),
    )
    mixed_time = (piece_add * lax.rsqrt(piece_sq / D + epsilon)[:, None, None, :]).astype(
        jnp.bfloat16
    )
    mixed_time = mixed_time.reshape(frames_all, 3, local_heads, HEAD_DIM, columns)
    time_scores = jnp.einsum(
        "fhep,ghep->hfgp", mixed_time[:, 0], mixed_time[:, 1], preferred_element_type=jnp.float32
    )
    time_weights = softmax_along(time_scores * HEAD_DIM ** (-0.5), 2)
    attended_time = jnp.einsum(
        "hfgp,ghep->fhep", time_weights, mixed_time[:, 2], preferred_element_type=jnp.float32
    )
    attended_time = attended_time.astype(jnp.bfloat16).reshape(frames_all, width, columns)
    update_time = add_mixed(
        lax.all_gather(attended_time, "heads", axis=1, tiled=True), temporal_out
    )
    block_out = (own_rows.astype(jnp.float32) + update_time).astype(jnp.bfloat16)
    returned = lax.all_to_all(block_out, "seq", split_axis=0, concat_axis=2, tiled=True)
    half_width = width // 2
    partner = from_partner(returned, "cfg", 0)
    branch_index = lax.axis_index("cfg")
    cond_full = jnp.where(branch_index == 0, returned, partner)
    uncond_full = jnp.where(branch_index == 0, partner, returned)
    cond_part = lax.dynamic_slice_in_dim(cond_full, branch_index * half_width, half_width, 1)
    uncond_part = lax.dynamic_slice_in_dim(uncond_full, branch_index * half_width, half_width, 1)
    ratio = guide_numer.astype(jnp.float32) / guide_denom.astype(jnp.float32)
    cond_wide = cond_part.astype(jnp.float32)
    uncond_wide = uncond_part.astype(jnp.float32)
    return (uncond_wide + ratio[:, None, None] * (cond_wide - uncond_wide)).astype(jnp.bfloat16)


def fits(mesh):
    heads = mesh.shape["heads"]
    share = mesh.shape["groups"] * mesh.shape["cfg"]
    return (D // (heads * share)) % (2 * HEAD_DIM) == 0


def aligned(offset, step=16):
    return pl.multiple_of(offset, step)


def weave(y, inverse, tail):
    heads = y.shape[0] // HEAD_DIM
    y = (y * inverse).reshape(heads, HEAD_DIM, y.shape[1])
    return jnp.concatenate([y, jnp.broadcast_to(tail, (heads,) + tail.shape)], axis=1)


def qkv_kernel(pieces, offs, *refs):
    video, refs = refs[:pieces], refs[pieces:]
    text, refs = refs[:pieces], refs[pieces:]
    gain, w, out, text_out, xs, ts = refs
    width = w.shape[1]

    def load(parts, scaled):
        total = None
        for r, part in enumerate(parts):
            rows = pl.ds(aligned(offs[r]), width)
            wide = part[...].astype(jnp.float32)
            scaled[rows, :] = (wide * gain[rows, :]).astype(jnp.bfloat16)
            sq = jnp.sum(wide * wide, axis=0, keepdims=True)
            total = sq if total is None else total + sq
        return lax.rsqrt(total / D + epsilon)

    def project(scaled, inverse, dest, kinds):
        count = scaled.shape[1]
        row = lax.broadcasted_iota(jnp.int32, (HEAD_ROWS - HEAD_DIM, count), 0)
        for slot, kind in enumerate(kinds):
            y = jnp.dot(w[kind], scaled[...], preferred_element_type=jnp.float32)
            tail = jnp.where((row == 0) & (kind == 2), 1.0, 0.0)
            dest[slot] = weave(y, inverse, tail).astype(jnp.bfloat16)

    @pl.when(pl.program_id(0) == 0)
    def _():
        project(ts, load(text, ts), text_out, (1, 2))

    project(xs, load(video, xs), out, (0, 1, 2))


def spatial_qkv_call(video, text, offs, gain, w):
    width, positions = video[0].shape
    tokens = text[0].shape[1]
    heads = width // HEAD_DIM
    block = min(256, positions)
    n = len(video)
    whole = lambda *shape: pl.BlockSpec(shape, lambda j, o: (0,) * len(shape))
    return pl.pallas_call(
        functools.partial(qkv_kernel, n),
        out_shape=(
            jax.ShapeDtypeStruct((3, heads, HEAD_ROWS, positions), jnp.bfloat16),
            jax.ShapeDtypeStruct((2, heads, HEAD_ROWS, tokens), jnp.bfloat16),
        ),
        grid_spec=pltpu.PrefetchScalarGridSpec(
            num_scalar_prefetch=1,
            grid=(positions // block,),
            in_specs=[pl.BlockSpec((width, block), lambda j, o: (0, j))] * n
            + [whole(width, tokens)] * n
            + [whole(D, 1), whole(3, width, D)],
            out_specs=[
                pl.BlockSpec((3, heads, HEAD_ROWS, block), lambda j, o: (0, 0, 0, j)),
                whole(2, heads, HEAD_ROWS, tokens),
            ],
            scratch_shapes=[
                pltpu.VMEM((D, block), jnp.bfloat16),
                pltpu.VMEM((D, tokens), jnp.bfloat16),
            ],
        ),
        compiler_params=pltpu.CompilerParams(vmem_limit_bytes=VMEM_LIMIT),
        cost_estimate=pl.CostEstimate(
            flops=6 * width * D * positions, bytes_accessed=12 * width * positions, transcendentals=0
        ),
    )(offs, *video, *text, gain, w)


def attend_kernel(info, q_ref, k_ref, v_ref, kt_ref, vt_ref, out):
    pair = q_ref.shape[1]
    rate = HEAD_DIM ** (-0.5) * 1.4426950408889634
    contract = (((0,), (0,)), ((), ()))
    results = []
    for i in range(pair):
        q = q_ref[0, i]
        s = lax.dot_general(k_ref[0, i], q, contract, preferred_element_type=jnp.float32)
        t = lax.dot_general(kt_ref[0, i], q, contract, preferred_element_type=jnp.float32)
        live = lax.broadcasted_iota(jnp.int32, t.shape, 0) < info[1]
        t = jnp.where(live, t, -jnp.inf)
        top = jnp.maximum(
            jnp.max(s, axis=0, keepdims=True), jnp.max(t, axis=0, keepdims=True)
        )
        e = jnp.exp2((s - top) * rate).astype(jnp.bfloat16)
        f = jnp.exp2((t - top) * rate).astype(jnp.bfloat16)
        o = jnp.dot(v_ref[0, i], e, preferred_element_type=jnp.float32)
        o = o + jnp.dot(vt_ref[0, i], f, preferred_element_type=jnp.float32)
        results.append(o[:HEAD_DIM] / o[HEAD_DIM : HEAD_DIM + 1])
    out[...] = jnp.concatenate(results, axis=0).astype(jnp.bfloat16)


def attend_call(info, qkv, text_kv, count):
    heads, positions = qkv.shape[1], qkv.shape[3]
    tokens = text_kv.shape[3]
    block = min(256, count)
    per = count // block
    pair = 2
    return pl.pallas_call(
        attend_kernel,
        out_shape=jax.ShapeDtypeStruct((heads * HEAD_DIM, count), jnp.bfloat16),
        grid_spec=pltpu.PrefetchScalarGridSpec(
            num_scalar_prefetch=1,
            grid=(heads // pair, per),
            in_specs=[
                pl.BlockSpec((1, pair, HEAD_ROWS, block), lambda i, j, o: (0, i, 0, o[0] * per + j)),
                pl.BlockSpec((1, pair, HEAD_ROWS, positions), lambda i, j, o: (1, i, 0, 0)),
                pl.BlockSpec((1, pair, HEAD_ROWS, positions), lambda i, j, o: (2, i, 0, 0)),
                pl.BlockSpec((1, pair, HEAD_ROWS, tokens), lambda i, j, o: (0, i, 0, 0)),
                pl.BlockSpec((1, pair, HEAD_ROWS, tokens), lambda i, j, o: (1, i, 0, 0)),
            ],
            out_specs=pl.BlockSpec((pair * HEAD_DIM, block), lambda i, j, o: (i, j)),
        ),
        compiler_params=pltpu.CompilerParams(vmem_limit_bytes=VMEM_LIMIT),
        cost_estimate=pl.CostEstimate(
            flops=16 * heads * HEAD_ROWS * count * positions,
            bytes_accessed=4 * heads * HEAD_ROWS * positions,
            transcendentals=heads * count * positions,
        ),
    )(info, qkv, qkv, qkv, text_kv, text_kv)


def out_kernel(n, blocks, info, *refs):
    att, refs = refs[:n], refs[n:]
    tokens, refs = refs[:n], refs[n:]
    w_own, refs = refs[0], refs[1:]
    w_far, (out, a) = refs[: len(blocks)], refs[len(blocks) :]
    width = w_own.shape[0]
    seq = out.shape[0]
    lanes = out.shape[2]
    for r in range(n):
        a[pl.ds(aligned(info[2 + r]), width), :] = att[r][...]

    def emit(y, base, offset):
        for j in range(seq):
            slot = lax.rem(j - info[1] + seq, seq)
            out[slot, pl.ds(aligned(base + offset), y.shape[0]), :] = y[
                :, j * lanes : (j + 1) * lanes
            ].astype(jnp.bfloat16)

    y = jnp.dot(w_own[...], a[...], preferred_element_type=jnp.float32)
    emit(y + tokens[0][...].astype(jnp.float32), info[2], 0)
    for b, (r, _, _) in enumerate(blocks):
        offset = info[2 + n + b]
        y = jnp.dot(w_far[b][...], a[...], preferred_element_type=jnp.float32)
        held = tokens[r][pl.ds(aligned(offset), y.shape[0]), :]
        emit(y + held.astype(jnp.float32), info[2 + r], offset)


def out_call(blocks, info, att, tokens, w_own, w_far, seq):
    n = len(att)
    width, count = att[0].shape
    whole = lambda x: pl.BlockSpec(x.shape, lambda i, o: (0,) * x.ndim)
    return pl.pallas_call(
        functools.partial(out_kernel, n, blocks),
        out_shape=jax.ShapeDtypeStruct((seq, D, count // seq), jnp.bfloat16),
        grid_spec=pltpu.PrefetchScalarGridSpec(
            num_scalar_prefetch=1,
            grid=(1,),
            in_specs=[whole(x) for x in att]
            + [pl.BlockSpec((width, count), lambda i, o: (0, o[0]))] * n
            + [whole(w_own)]
            + [whole(x) for x in w_far],
            out_specs=pl.BlockSpec((seq, D, count // seq), lambda i, o: (0, 0, 0)),
            scratch_shapes=[pltpu.VMEM((D, count), jnp.bfloat16)],
        ),
        compiler_params=pltpu.CompilerParams(vmem_limit_bytes=VMEM_LIMIT),
        cost_estimate=pl.CostEstimate(
            flops=2 * D * D * count, bytes_accessed=8 * D * count, transcendentals=0
        ),
    )(info, *att, *tokens, w_own, *w_far)


def time_kernel(frames, blocks, share, info, *refs):
    state, refs = refs[0], refs[1:]
    far_state, refs = refs[: frames - 1], refs[frames - 1 :]
    gain, w_own, o_own, refs = refs[0], refs[1], refs[2], refs[3:]
    w_far, refs = refs[: len(blocks)], refs[len(blocks) :]
    o_far, refs = refs[: len(blocks)], refs[len(blocks) :]
    keep, send, xs, att, res, wbuf, obuf, wsem, osem = refs
    lanes = state.shape[2]
    rows = obuf.shape[1]
    total = share + len(blocks)
    heads = rows // HEAD_DIM

    def w_copy(b):
        source = w_own.at[:, pl.ds(b * rows, rows), :] if b < share else w_far[b - share]
        return pltpu.make_async_copy(source, wbuf.at[b], wsem.at[b])

    def o_copy(b):
        source = o_own.at[pl.ds(b * rows, rows), :] if b < share else o_far[b - share]
        return pltpu.make_async_copy(source, obuf.at[b], osem.at[b])

    for b in range(total):
        w_copy(b).start()
    for b in range(total):
        o_copy(b).start()

    inverses = []
    for f in range(frames):
        x = (state[0] if f == 0 else far_state[f - 1][...]).astype(jnp.float32)
        cols = slice(f * lanes, (f + 1) * lanes)
        xs[:, cols] = (x * gain[...]).astype(jnp.bfloat16)
        inverses.append(lax.rsqrt(jnp.sum(x * x, axis=0, keepdims=True) / D + epsilon))
    inverse = jnp.concatenate(inverses, axis=1)

    for b in range(total):
        w_copy(b).wait()
        parts = []
        for kind in range(3):
            y = jnp.dot(wbuf[b, kind], xs[...], preferred_element_type=jnp.float32)
            y = (y * inverse).astype(jnp.bfloat16).astype(jnp.float32)
            parts.append(
                [
                    y[:, f * lanes : (f + 1) * lanes].reshape(heads, HEAD_DIM, lanes)
                    for f in range(frames)
                ]
            )
        query, key, value = parts
        for f in range(frames):
            scores = [
                jnp.sum(query[f] * key[g], axis=1, keepdims=True) * HEAD_DIM ** (-0.5)
                for g in range(frames)
            ]
            top = functools.reduce(jnp.maximum, scores)
            expons = [jnp.exp(score - top) for score in scores]
            bottom = functools.reduce(jnp.add, expons)
            result = None
            for g in range(frames):
                weight = (expons[g] / bottom).astype(jnp.bfloat16).astype(jnp.float32)
                term = weight * value[g]
                result = term if result is None else result + term
            att[pl.ds(aligned(info[4 + b]), rows), f * lanes : (f + 1) * lanes] = result.reshape(
                rows, lanes
            ).astype(jnp.bfloat16)

    for b in range(total):
        o_copy(b).wait()
        y = jnp.dot(obuf[b], att[...], preferred_element_type=jnp.float32)
        span = pl.ds(aligned(info[4 + b]), rows)
        for f in range(frames):
            x = state[0, span, :] if f == 0 else far_state[f - 1][span, :]
            res[f, span, :] = (
                x.astype(jnp.float32) + y[:, f * lanes : (f + 1) * lanes]
            ).astype(jnp.bfloat16)

    parts = keep.shape[1]
    slot_rows = keep.shape[2]
    for f in range(frames):
        for r in range(parts):
            head = lax.rem(info[0] + r, parts)
            keep[f, r] = res[f, pl.ds(aligned((head * 2 + info[1]) * slot_rows), slot_rows), :]
            send[f, r] = res[f, pl.ds(aligned((head * 2 + 1 - info[1]) * slot_rows), slot_rows), :]


def time_call(blocks, share, parts, info, state, far_state, gain, w_own, o_own, w_far, o_far):
    frames, lanes = state.shape[0], state.shape[2]
    rows = w_far[0].shape[1]
    total = share + len(blocks)
    whole = lambda x: pl.BlockSpec(x.shape, lambda i, o: (0,) * x.ndim)
    anywhere = pl.BlockSpec(memory_space=pl.ANY)
    result = jax.ShapeDtypeStruct((frames, parts, D // (2 * parts), lanes), jnp.bfloat16)
    return pl.pallas_call(
        functools.partial(time_kernel, frames, blocks, share),
        out_shape=(result, result),
        grid_spec=pltpu.PrefetchScalarGridSpec(
            num_scalar_prefetch=1,
            grid=(1,),
            in_specs=[whole(state)]
            + [whole(x) for x in far_state]
            + [whole(gain)]
            + [anywhere] * (2 + len(w_far) + len(o_far)),
            out_specs=[whole(result), whole(result)],
            scratch_shapes=[
                pltpu.VMEM((D, frames * lanes), jnp.bfloat16),
                pltpu.VMEM((D, frames * lanes), jnp.bfloat16),
                pltpu.VMEM((frames, D, lanes), jnp.bfloat16),
                pltpu.VMEM((total, 3, rows, D), jnp.bfloat16),
                pltpu.VMEM((total, rows, D), jnp.bfloat16),
                pltpu.SemaphoreType.DMA((total,)),
                pltpu.SemaphoreType.DMA((total,)),
            ],
        ),
        compiler_params=pltpu.CompilerParams(vmem_limit_bytes=VMEM_LIMIT),
        cost_estimate=pl.CostEstimate(
            flops=8 * D * D * frames * lanes, bytes_accessed=8 * D * D, transcendentals=0
        ),
    )(info, state, *far_state, gain, w_own, o_own, *w_far, *o_far)


def place_kernel(n, offs, *refs):
    out = refs[n]
    for i in range(n):
        piece = refs[i]
        span = pl.ds(aligned(offs[i], LANES), piece.shape[1])
        out[:, span] = piece[...]


def place_call(offs, pieces):
    rows, lanes = pieces[0].shape
    n = len(pieces)
    whole = pl.BlockSpec((rows, lanes), lambda i, o: (0, 0))
    return pl.pallas_call(
        functools.partial(place_kernel, n),
        out_shape=jax.ShapeDtypeStruct((rows, n * lanes), jnp.bfloat16),
        grid_spec=pltpu.PrefetchScalarGridSpec(
            num_scalar_prefetch=1,
            grid=(1,),
            in_specs=[whole] * n,
            out_specs=pl.BlockSpec((rows, n * lanes), lambda i, o: (0, 0)),
        ),
        compiler_params=pltpu.CompilerParams(vmem_limit_bytes=VMEM_LIMIT),
    )(offs, *pieces)


def shift(x, axis, by):
    size = lax.axis_size(axis)
    return lax.ppermute(x, axis, [(i, (i + by) % size) for i in range(size)])


def after(x, *gates):
    return lax.optimization_barrier((x,) + gates)[0]


def share_rows(w, blocks, gate):
    rows = w.shape[-2] // (lax.axis_size("groups") * lax.axis_size("cfg"))
    own = lax.axis_index("groups") * lax.axis_size("cfg") + lax.axis_index("cfg")
    mine = lax.dynamic_slice_in_dim(w, own * rows, rows, w.ndim - 2)
    mine = after(mine, *gate)
    held = {}
    for r, dg, dc in blocks:
        if dc:
            held[r, dg, dc] = shift(held[r, dg, 0], "cfg", dc)
        elif dg:
            held[r, dg, dc] = shift(held[r, 0, 0], "groups", dg)
        else:
            held[r, dg, dc] = shift(mine, "heads", r)
    return [held[b] for b in blocks]


def shards(fit, *args):
    (
        video_tokens,
        text_tokens,
        text_length,
        guide_numer,
        guide_denom,
        spatial_gain,
        spatial_qkv,
        spatial_out,
        temporal_gain,
        temporal_qkv,
        temporal_out,
    ) = args
    heads, seq = lax.axis_size("heads"), lax.axis_size("seq")
    groups, cfg = lax.axis_size("groups"), lax.axis_size("cfg")
    positions = video_tokens.shape[3]
    lanes = positions // (heads * seq)
    if not fit or lanes % LANES or video_tokens.shape[1] != 1:
        return shards_plain(*args)
    h, s = lax.axis_index("heads"), lax.axis_index("seq")
    g, c = lax.axis_index("groups"), lax.axis_index("cfg")
    video, text = video_tokens[0, 0], text_tokens[0, 0]
    width = video.shape[0]
    count = positions // heads
    share = groups * cfg
    rows = width // share
    blocks = [
        (r, dg, dc) for r in range(1, heads) for dg in range(groups) for dc in range(cfg)
    ]
    gain_one = spatial_gain.astype(jnp.float32)[:, None]
    gain_two = temporal_gain.astype(jnp.float32)[:, None]

    video_all = [video] + [shift(video, "heads", r) for r in range(1, heads)]
    text_all = [text] + [shift(text, "heads", r) for r in range(1, heads)]
    bases = [lax.rem(h - r + heads, heads) * width for r in range(heads)]
    quarter = {
        (r, dg, dc): (
            lax.rem(g - dg + groups, groups) * cfg + lax.rem(c - dc + cfg, cfg)
        )
        * rows
        for r, dg, dc in blocks
    }
    qkv, text_kv = spatial_qkv_call(
        video_all, text_all, jnp.stack(bases).astype(jnp.int32), gain_one, spatial_qkv
    )
    out_far = share_rows(spatial_out, blocks, video_all[1:])
    last_far = share_rows(temporal_out, blocks, video_all[1:] + out_far)

    att = {}
    for r in list(range(1, heads)) + [0]:
        info = jnp.stack([lax.rem(h + r, heads), text_length[0, 0]]).astype(jnp.int32)
        att[r] = attend_call(info, qkv, text_kv, count)
        if r:
            att[r] = shift(att[r], "heads", r)
    att_all = [att[r] for r in range(heads)]
    time_far = share_rows(temporal_qkv, blocks, att_all[1:])

    info = jnp.stack([h, s] + bases + [quarter[b] for b in blocks]).astype(jnp.int32)
    state = out_call(blocks, info, att_all, video_all, spatial_out, out_far, seq)
    far_state = [shift(state[k], "seq", k) for k in range(1, seq)]

    starts = [bases[0] + q * rows for q in range(share)]
    starts += [bases[b[0]] + quarter[b] for b in blocks]
    info = jnp.stack([h, c, s, g] + starts).astype(jnp.int32)
    keep, send = time_call(
        blocks,
        share,
        heads,
        info,
        state,
        far_state,
        gain_two,
        temporal_qkv,
        temporal_out,
        time_far,
        last_far,
    )
    other = shift(send, "cfg", 1)
    ratio = guide_numer.astype(jnp.float32) / guide_denom.astype(jnp.float32)
    ratios = jnp.stack([ratio] + [shift(ratio, "seq", k) for k in range(1, seq)])
    keep_wide, other_wide = keep.astype(jnp.float32), other.astype(jnp.float32)
    cond = jnp.where(c == 0, keep_wide, other_wide)
    uncond = jnp.where(c == 0, other_wide, keep_wide)
    guided = (uncond + ratios[:, :, None, None] * (cond - uncond)).astype(jnp.bfloat16)

    pieces, places = [], []
    for k in range(seq):
        for r in range(heads):
            piece = guided[k, r]
            if k or r:
                route = [
                    (a * heads + b, (a - k) % seq * heads + (b + r) % heads)
                    for a in range(seq)
                    for b in range(heads)
                ]
                piece = lax.ppermute(piece, ("seq", "heads"), route)
            pieces.append(piece)
            place = lax.rem(h - r + heads, heads) * seq + lax.rem(s + k, seq)
            places.append(place * lanes)
    return place_call(jnp.stack(places).astype(jnp.int32), pieces)[None]


def solution(mesh):
    return jax.shard_map(
        functools.partial(shards, fits(mesh)),
        mesh=mesh,
        in_specs=(
            P("cfg", ("groups", "seq"), "heads", None),
            P("cfg", ("groups", "seq"), "heads", None),
            P("cfg", ("groups", "seq")),
            P(("groups", "seq")),
            P(("groups", "seq")),
            P(),
            P(None, "heads", None),
            P("heads", None),
            P(),
            P(None, "heads", None),
            P("heads", None),
        ),
        out_specs=P(("groups", "seq"), ("heads", "cfg"), None),
        check_vma=False,
    )
```

```python
import functools

import jax
import jax.numpy as jnp
from jax import lax
from jax.experimental import pallas as pl
from jax.experimental.pallas import tpu as pltpu
from jax.sharding import PartitionSpec as P

D = 1152
HEAD_DIM = 72
HEAD_ROWS = 80
LANES = 128


epsilon = 1e-06


def from_partner(shard, axis, stride):
    return lax.ppermute(shard, axis, [(i, i ^ 1 << stride) for i in range(lax.axis_size(axis))])


def softmax_along(scores, axis):
    top_score = jnp.max(scores, axis=axis, keepdims=True)
    expons = jnp.exp(scores - top_score)
    return (expons / jnp.sum(expons, axis=axis, keepdims=True)).astype(jnp.bfloat16)


def project_piece(piece, gain_vector, weights, parts):
    gain_piece = gain_vector.astype(jnp.float32)
    weight_piece = weights[parts]
    piece_wide = piece.astype(jnp.float32)
    scaled = (piece_wide * gain_piece[None, :, None]).astype(jnp.bfloat16)
    product = jnp.einsum("kod,fdp->fkop", weight_piece, scaled, preferred_element_type=jnp.float32)
    return (product, jnp.sum(piece_wide * piece_wide, axis=1))


def add_mixed(piece, matrix):
    return jnp.einsum("oc,fcp->fop", matrix, piece, preferred_element_type=jnp.float32)


def shards_plain(
    video_tokens,
    text_tokens,
    text_length,
    guide_numer,
    guide_denom,
    spatial_gain,
    spatial_qkv,
    spatial_out,
    temporal_gain,
    temporal_qkv,
    temporal_out,
):
    frame_count = video_tokens.shape[1]
    width = video_tokens.shape[2]
    positions = video_tokens.shape[3]
    text_count = text_tokens.shape[3]
    local_heads = width // HEAD_DIM
    frame_tokens = video_tokens[0]
    frame_text = text_tokens[0]
    video_piece = lax.all_gather(frame_tokens, "heads", axis=1, tiled=True)
    text_piece = lax.all_gather(frame_text, "heads", axis=1, tiled=True)
    video_add, video_sq = project_piece(video_piece, spatial_gain, spatial_qkv, slice(0, 3))
    text_add, text_sq = project_piece(text_piece, spatial_gain, spatial_qkv, slice(1, 3))
    mixed = (video_add * lax.rsqrt(video_sq / D + epsilon)[:, None, None, :]).astype(jnp.bfloat16)
    mixed = mixed.reshape(frame_count, 3, local_heads, HEAD_DIM, positions)
    context = (text_add * lax.rsqrt(text_sq / D + epsilon)[:, None, None, :]).astype(jnp.bfloat16)
    context = context.reshape(frame_count, 2, local_heads, HEAD_DIM, text_count)
    key_rows = jnp.concatenate([mixed[:, 1], context[:, 0]], axis=3)
    value_rows = jnp.concatenate([mixed[:, 2], context[:, 1]], axis=3)
    query_all = mixed[:, 0]
    text_valid = jnp.arange(text_count, dtype=jnp.int32)[None, :] < text_length[0][:, None]
    valid_keys = jnp.concatenate(
        [jnp.ones((frame_count, positions), dtype=bool), text_valid], axis=1
    )
    block_rows = min(512, positions)
    block_count = positions // block_rows
    frame_ids = jnp.repeat(jnp.arange(frame_count, dtype=jnp.int32), block_count)
    block_ids = jnp.tile(jnp.arange(block_count, dtype=jnp.int32), frame_count)

    def block_step(inputs):
        frame_id, block_id = inputs
        query_rows = lax.dynamic_slice_in_dim(
            query_all[frame_id], block_id * block_rows, block_rows, 2
        )
        scores = jnp.einsum(
            "hep,hek->hpk", query_rows, key_rows[frame_id], preferred_element_type=jnp.float32
        )
        scores = scores * HEAD_DIM ** (-0.5)
        scores = jnp.where(valid_keys[frame_id][None, None, :], scores, -jnp.inf)
        weights = softmax_along(scores, 2)
        result = jnp.einsum(
            "hpk,hek->hep", weights, value_rows[frame_id], preferred_element_type=jnp.float32
        )
        return result.astype(jnp.bfloat16)

    attended = lax.map(block_step, (frame_ids, block_ids))
    attended = attended.reshape(frame_count, block_count, local_heads, HEAD_DIM, block_rows)
    attended = jnp.transpose(attended, (0, 2, 3, 1, 4)).reshape(frame_count, width, positions)
    update = add_mixed(lax.all_gather(attended, "heads", axis=1, tiled=True), spatial_out)
    after_spatial = (frame_tokens.astype(jnp.float32) + update).astype(jnp.bfloat16)
    own_rows = lax.all_to_all(after_spatial, "seq", split_axis=2, concat_axis=0, tiled=True)
    frames_all = own_rows.shape[0]
    columns = own_rows.shape[2]
    piece_add, piece_sq = project_piece(
        lax.all_gather(own_rows, "heads", axis=1, tiled=True),
        temporal_gain,
        temporal_qkv,
        slice(0, 3),
    )
    mixed_time = (piece_add * lax.rsqrt(piece_sq / D + epsilon)[:, None, None, :]).astype(
        jnp.bfloat16
    )
    mixed_time = mixed_time.reshape(frames_all, 3, local_heads, HEAD_DIM, columns)
    time_scores = jnp.einsum(
        "fhep,ghep->hfgp", mixed_time[:, 0], mixed_time[:, 1], preferred_element_type=jnp.float32
    )
    time_weights = softmax_along(time_scores * HEAD_DIM ** (-0.5), 2)
    attended_time = jnp.einsum(
        "hfgp,ghep->fhep", time_weights, mixed_time[:, 2], preferred_element_type=jnp.float32
    )
    attended_time = attended_time.astype(jnp.bfloat16).reshape(frames_all, width, columns)
    update_time = add_mixed(
        lax.all_gather(attended_time, "heads", axis=1, tiled=True), temporal_out
    )
    block_out = (own_rows.astype(jnp.float32) + update_time).astype(jnp.bfloat16)
    returned = lax.all_to_all(block_out, "seq", split_axis=0, concat_axis=2, tiled=True)
    half_width = width // 2
    partner = from_partner(returned, "cfg", 0)
    branch_index = lax.axis_index("cfg")
    cond_full = jnp.where(branch_index == 0, returned, partner)
    uncond_full = jnp.where(branch_index == 0, partner, returned)
    cond_part = lax.dynamic_slice_in_dim(cond_full, branch_index * half_width, half_width, 1)
    uncond_part = lax.dynamic_slice_in_dim(uncond_full, branch_index * half_width, half_width, 1)
    ratio = guide_numer.astype(jnp.float32) / guide_denom.astype(jnp.float32)
    cond_wide = cond_part.astype(jnp.float32)
    uncond_wide = uncond_part.astype(jnp.float32)
    return (uncond_wide + ratio[:, None, None] * (cond_wide - uncond_wide)).astype(jnp.bfloat16)


def fits(mesh):
    heads = mesh.shape["heads"]
    share = mesh.shape["groups"] * mesh.shape["cfg"]
    return (D // (heads * share)) % (2 * HEAD_DIM) == 0


def aligned(offset, step=16):
    return pl.multiple_of(offset, step)


def local(x):
    return pltpu.with_memory_space_constraint(x, pltpu.VMEM)


def resident(kernel, shapes, info, operands, scratch, flops, grant, exps=0, out_local=True):
    place = pl.BlockSpec(memory_space=pltpu.VMEM)
    kind = pltpu.VMEM if out_local else jax.ShapeDtypeStruct
    moved = sum(x.size * x.dtype.itemsize for x in operands)
    return pl.pallas_call(
        kernel,
        out_shape=tuple(kind(shape, dtype) for shape, dtype in shapes),
        in_specs=[pl.BlockSpec(memory_space=pltpu.SMEM)] + [place] * len(operands),
        out_specs=(place,) * len(shapes),
        scratch_shapes=scratch,
        compiler_params=pltpu.CompilerParams(vmem_limit_bytes=grant << 20),
        cost_estimate=pl.CostEstimate(flops=flops, bytes_accessed=moved, transcendentals=exps),
    )(info, *[local(x) for x in operands])


def place_of(axis):
    return lax.axis_index(axis)


def base_of(heads, r, width):
    return lax.rem(place_of("heads") - r + heads, heads) * width


def quarter_of(block, rows, groups, cfg):
    _, dg, dc = block
    g = lax.rem(place_of("groups") - dg + groups, groups)
    return (g * cfg + lax.rem(place_of("cfg") - dc + cfg, cfg)) * rows


def weave(y, inverse, tail):
    heads = y.shape[0] // HEAD_DIM
    y = (y * inverse).reshape(heads, HEAD_DIM, y.shape[1])
    return jnp.concatenate([y, jnp.broadcast_to(tail, (heads,) + tail.shape)], axis=1)


def project_kernel(parts, jobs, info, *refs):
    inputs, refs = refs[: parts * len(jobs)], refs[parts * len(jobs) :]
    gain, w, refs = refs[0], refs[1], refs[2:]
    outs, scaled_refs = refs[: len(jobs)], refs[len(jobs) :]
    width = w.shape[1]
    for i, kinds in enumerate(jobs):
        scaled, total = scaled_refs[i], None
        for r in range(parts):
            rows = pl.ds(aligned(base_of(parts, r, width)), width)
            wide = inputs[i * parts + r][...].astype(jnp.float32)
            scaled[rows, :] = (wide * gain[rows, :]).astype(jnp.bfloat16)
            sq = jnp.sum(wide * wide, axis=0, keepdims=True)
            total = sq if total is None else total + sq
        inverse = lax.rsqrt(total / D + epsilon)
        row = lax.broadcasted_iota(
            jnp.int32, (HEAD_ROWS - HEAD_DIM, scaled.shape[1]), 0
        )
        for slot, kind in enumerate(kinds):
            y = jnp.dot(w[kind], scaled[...], preferred_element_type=jnp.float32)
            tail = jnp.where((row == 0) & (kind == 2), 1.0, 0.0)
            outs[i][slot] = weave(y, inverse, tail).astype(jnp.bfloat16)


def project_call(info, sets, jobs, gain, w):
    width = w.shape[1]
    heads = width // HEAD_DIM
    parts = len(sets[0])
    counts = [x[0].shape[1] for x in sets]
    shapes = [
        ((len(kinds), heads, HEAD_ROWS, n), jnp.bfloat16) for kinds, n in zip(jobs, counts)
    ]
    return resident(
        functools.partial(project_kernel, parts, jobs),
        shapes,
        info,
        [x for group in sets for x in group] + [gain, w],
        [pltpu.VMEM((D, n), jnp.bfloat16) for n in counts],
        6 * width * D * sum(counts),
        12,
    )


def attend_kernel(n, heads_axis, ahead, info, *refs):
    chunks, (text, out, s_buf, m_buf, o_buf) = refs[:n], refs[n:]
    heads, block = chunks[0].shape[1], chunks[0].shape[3]
    per = out.shape[1] // block
    half = lax.rem(place_of("heads") + ahead, heads_axis)
    rate = HEAD_DIM ** (-0.5) * 1.4426950408889634
    contract = (((0,), (0,)), ((), ()))

    def fold(s):
        return jnp.max(s.reshape(s.shape[0] // 8, 8, s.shape[1]), axis=0)

    def score(head, j, slot):
        q = chunks[j][0, head]
        for b in range(1, heads_axis):
            q = jnp.where(half == b, chunks[b * per + j][0, head], q)
        top = None
        for i, chunk in enumerate(chunks):
            s = lax.dot_general(chunk[1, head], q, contract, preferred_element_type=jnp.float32)
            s_buf[slot, i * block : (i + 1) * block, :] = s
            top = fold(s) if top is None else jnp.maximum(top, fold(s))
        t = lax.dot_general(text[0, head], q, contract, preferred_element_type=jnp.float32)
        live = lax.broadcasted_iota(jnp.int32, t.shape, 0) < info[0]
        t = jnp.where(live, t, -jnp.inf)
        s_buf[slot, n * block :, :] = t
        m_buf[slot] = jnp.maximum(top, fold(t))

    def mix(head, j, slot):
        top = jnp.max(m_buf[slot], axis=0, keepdims=True)
        o = None
        for i in range(n + 1):
            if i < n:
                s, v = s_buf[slot, i * block : (i + 1) * block, :], chunks[i][2, head]
            else:
                s, v = s_buf[slot, n * block :, :], text[1, head]
            e = jnp.exp2((s - top) * rate).astype(jnp.bfloat16)
            term = jnp.dot(v, e, preferred_element_type=jnp.float32)
            o = term if o is None else o + term
        rows = pl.ds(aligned(head * HEAD_DIM, 8), HEAD_DIM)
        o_buf[rows, j * block : (j + 1) * block] = o[:HEAD_DIM] / o[HEAD_DIM : HEAD_DIM + 1]

    score(0, 0, 0)

    def step(head, carry):
        for j in range(per):
            if j + 1 < per:
                score(head, j + 1, (j + 1) % 2)
            else:
                score(head + 1, 0, 0)
            mix(head, j, j % 2)
        return carry

    lax.fori_loop(0, heads - 1, step, 0)
    for j in range(per):
        if j + 1 < per:
            score(heads - 1, j + 1, (j + 1) % 2)
        mix(heads - 1, j, j % 2)
    out[...] = o_buf[...].astype(jnp.bfloat16)


def attend_call(info, chunks, text, heads_axis, ahead):
    _, heads, _, block = chunks[0].shape
    count = block * len(chunks) // heads_axis
    keys = block * len(chunks) + text.shape[3]
    return resident(
        functools.partial(attend_kernel, len(chunks), heads_axis, ahead),
        [((heads * HEAD_DIM, count), jnp.bfloat16)],
        info,
        list(chunks) + [text],
        [
            pltpu.VMEM((2, keys, block), jnp.float32),
            pltpu.VMEM((2, 8, block), jnp.float32),
            pltpu.VMEM((heads * HEAD_DIM, count), jnp.float32),
        ],
        4 * heads * 256 * count * keys,
        8,
        heads * count * keys,
    )[0]


def out_kernel(n, per, extra, seq, blocks, share, info, *refs):
    att, refs = refs[:n], refs[n:]
    tokens, refs = refs[: per * n * len(blocks)], refs[per * n * len(blocks) :]
    w, refs = refs[: len(blocks)], refs[len(blocks) :]
    outs, (a, held) = refs[:seq], refs[seq:]
    width = att[0].shape[0]
    lanes = outs[0].shape[1]
    block = tokens[0].shape[1]
    half, frame = place_of("heads"), place_of("seq")
    for r in range(n):
        a[pl.ds(aligned(base_of(n, r, width)), width), :] = att[r][...]
    for b, key in enumerate(blocks):
        y = jnp.dot(w[b][...], a[...], preferred_element_type=jnp.float32)
        count = y.shape[0]
        if count == width:
            inner, rows = slice(0, width), slice(0, width)
        else:
            offset = aligned(quarter_of(key, count, *share))
            inner, rows = pl.ds(offset, count), pl.ds(aligned((key[0] - 1) * width + offset), count)
        for j in range(per):
            x = tokens[(b * n) * per + j][inner, :]
            for i in range(1, n):
                x = jnp.where(half == i, tokens[(b * n + i) * per + j][inner, :], x)
            cols = slice(j * block, (j + 1) * block)
            held[rows, cols] = (x.astype(jnp.float32) + y[:, cols]).astype(jnp.bfloat16)
    total = held.shape[0]
    for k in range(seq):
        dest = lax.rem(frame + k, seq)
        outs[k][0:total, :] = held[:, pl.ds(aligned(dest * lanes, LANES), lanes)]
        if extra:
            row = lax.broadcasted_iota(jnp.int32, (extra, lanes), 0)
            numer, denom = info[1].astype(jnp.float32), info[2].astype(jnp.float32)
            tail = jnp.where(row == 0, numer, jnp.where(row == 1, denom, 0.0))
            outs[k][total:, :] = tail.astype(jnp.bfloat16)


def out_call(info, att, tokens, w, per, extra, seq, total, blocks, share):
    n = len(att)
    count = att[0].shape[1]
    return resident(
        functools.partial(out_kernel, n, per, extra, seq, blocks, share),
        [((total + extra, count // seq), jnp.bfloat16)] * seq,
        info,
        list(att) + [x for group in tokens for x in group] + list(w),
        [pltpu.VMEM((D, count), jnp.bfloat16), pltpu.VMEM((total, count), jnp.bfloat16)],
        2 * D * total * count,
        12,
    )


def time_kernel(frames, parts, groups, cfg, keys, info, *refs):
    blocks, share = len(keys), groups * cfg
    near, refs = refs[:frames], refs[frames:]
    far, refs = refs[:frames], refs[frames:]
    gain, w_own, o_own, refs = refs[0], refs[1], refs[2], refs[3:]
    w_far, refs = refs[: 3 * blocks], refs[3 * blocks :]
    o_far, refs = refs[:blocks], refs[blocks:]
    keep, send, ratios, xs, att, res = refs
    lanes = near[0].shape[1]
    width = w_own.shape[1]
    rows = width // share
    heads = rows // HEAD_DIM
    head_index, branch = place_of("heads"), place_of("cfg")
    offsets = [base_of(parts, 0, width) + q * rows for q in range(share)]
    offsets += [
        base_of(parts, key[0], width) + quarter_of(key, rows, groups, cfg) for key in keys
    ]

    def w_of(b, kind):
        if b < share:
            return w_own[kind, b * rows : (b + 1) * rows, :]
        return w_far[3 * (b - share) + kind][...]

    def o_of(b):
        if b < share:
            return o_own[b * rows : (b + 1) * rows, :]
        return o_far[b - share][...]

    inverses = []
    for f in range(frames):
        cols = slice(f * lanes, (f + 1) * lanes)
        total = None
        for r in range(parts):
            base = base_of(parts, r, width)
            span = pl.ds(aligned(base), width)
            if r == 0:
                x = near[f][0:width, :]
            else:
                x = far[f][(r - 1) * width : r * width, :]
            res[f, span, :] = x
            x = x.astype(jnp.float32)
            xs[span, cols] = (x * gain[pl.ds(aligned(D + base), width), :]).astype(jnp.bfloat16)
            sq = jnp.sum(x * x, axis=0, keepdims=True)
            total = sq if total is None else total + sq
        inverses.append(lax.rsqrt(total / D + epsilon))
        tail = near[f][width:, :].astype(jnp.float32)
        ratios[f : f + 1, :] = tail[0:1] / tail[1:2]
    inverse = jnp.concatenate(inverses, axis=1)

    for b in range(share + blocks):
        split = []
        for kind in range(3):
            y = jnp.dot(w_of(b, kind), xs[...], preferred_element_type=jnp.float32)
            y = (y * inverse).astype(jnp.bfloat16).astype(jnp.float32)
            split.append(
                [
                    y[:, f * lanes : (f + 1) * lanes].reshape(heads, HEAD_DIM, lanes)
                    for f in range(frames)
                ]
            )
        query, key, value = split
        for f in range(frames):
            scores = [
                jnp.sum(query[f] * key[g], axis=1, keepdims=True) * HEAD_DIM ** (-0.5)
                for g in range(frames)
            ]
            top = functools.reduce(jnp.maximum, scores)
            expons = [jnp.exp(x - top) for x in scores]
            bottom = functools.reduce(jnp.add, expons)
            result = None
            for g in range(frames):
                weight = (expons[g] / bottom).astype(jnp.bfloat16).astype(jnp.float32)
                term = weight * value[g]
                result = term if result is None else result + term
            att[pl.ds(aligned(offsets[b]), rows), f * lanes : (f + 1) * lanes] = (
                result.reshape(rows, lanes).astype(jnp.bfloat16)
            )

    for b in range(share + blocks):
        y = jnp.dot(o_of(b), att[...], preferred_element_type=jnp.float32)
        span = pl.ds(aligned(offsets[b]), rows)
        for f in range(frames):
            x = res[f, span, :].astype(jnp.float32) + y[:, f * lanes : (f + 1) * lanes]
            res[f, span, :] = x.astype(jnp.bfloat16)

    slot = keep.shape[2]
    for f in range(frames):
        for r in range(parts):
            head = lax.rem(head_index + r, parts)
            keep[f, r] = res[f, pl.ds(aligned((head * 2 + branch) * slot), slot), :]
            send[f, r] = res[f, pl.ds(aligned((head * 2 + 1 - branch) * slot), slot), :]


def time_call(info, near, far, gain, w_own, o_own, w_far, o_far, parts, groups, cfg, keys):
    frames, lanes = len(near), near[0].shape[1]
    result = ((frames, parts, D // (2 * parts), lanes), jnp.bfloat16)
    return resident(
        functools.partial(time_kernel, frames, parts, groups, cfg, keys),
        [result, result, ((frames, lanes), jnp.float32)],
        info,
        list(near) + list(far) + [gain, w_own, o_own] + list(w_far) + list(o_far),
        [
            pltpu.VMEM((D, frames * lanes), jnp.bfloat16),
            pltpu.VMEM((D, frames * lanes), jnp.bfloat16),
            pltpu.VMEM((frames, D, lanes), jnp.bfloat16),
        ],
        8 * D * D * frames * lanes,
        12,
    )


def guide_kernel(info, keep, other, ratios, *outs):
    frames, parts = keep.shape[0], keep.shape[1]
    branch = place_of("cfg")
    for f in range(frames):
        ratio = ratios[f : f + 1, :]
        for r in range(parts):
            mine = keep[f, r].astype(jnp.float32)
            theirs = other[f, r].astype(jnp.float32)
            cond = jnp.where(branch == 0, mine, theirs)
            uncond = jnp.where(branch == 0, theirs, mine)
            outs[f * parts + r][...] = (uncond + ratio * (cond - uncond)).astype(jnp.bfloat16)


def place_kernel(seq, parts, info, *refs):
    out = refs[seq * parts]
    head, frame = place_of("heads"), place_of("seq")
    for k in range(seq):
        for r in range(parts):
            piece = refs[k * parts + r]
            slot = lax.rem(head - r + parts, parts) * seq + lax.rem(frame + k, seq)
            lanes = piece.shape[1]
            out[:, pl.ds(aligned(slot * lanes, LANES), lanes)] = piece[...]


def pick_kernel(groups, cfg, *refs):
    count = len(refs) // 2
    sources, outs, sems = refs[:count], refs[count : 2 * count], refs[2 * count]
    copies = []
    for i, (source, out) in enumerate(zip(sources, outs)):
        rows = out.shape[-2]
        span = pl.ds(aligned(quarter_of((0, 0, 0), rows, groups, cfg)), rows)
        view = source.at[:, span, :] if len(source.shape) == 3 else source.at[span, :]
        copies.append(pltpu.make_async_copy(view, out, sems.at[i]))
    for copy in copies:
        copy.start()
    for copy in copies:
        copy.wait()


def shift(x, axis, by):
    size = lax.axis_size(axis)
    return lax.ppermute(x, axis, [(i, (i + by) % size) for i in range(size)])


def after(x, *gates):
    return lax.optimization_barrier((x,) + gates)[0]


def shards(fit, *args):
    (video_tokens, _, _, _, _, _, _, _, _, _, _) = args
    heads, seq = lax.axis_size("heads"), lax.axis_size("seq")
    positions = video_tokens.shape[3]
    lanes = positions // (heads * seq)
    if not fit or lanes % LANES or seq % 2 or video_tokens.shape[1] != 1:
        return shards_plain(*args)
    return shards_fast(*args)


def shards_fast(
    video_tokens,
    text_tokens,
    text_length,
    guide_numer,
    guide_denom,
    spatial_gain,
    spatial_qkv,
    spatial_out,
    temporal_gain,
    temporal_qkv,
    temporal_out,
):
    heads, seq = lax.axis_size("heads"), lax.axis_size("seq")
    groups, cfg = lax.axis_size("groups"), lax.axis_size("cfg")
    positions = video_tokens.shape[3]
    lanes = positions // (heads * seq)
    video, text = video_tokens[0, 0], text_tokens[0, 0]
    width = video.shape[0]
    rows = width // (groups * cfg)
    per = 2
    block = positions // (heads * per)
    ring = range(1, heads)
    info = jnp.concatenate([text_length[0], guide_numer, guide_denom])
    gain = jnp.concatenate([spatial_gain, temporal_gain]).astype(jnp.float32)[:, None]

    text_set = [text] + [shift(text, "heads", r) for r in ring]
    chunk_sets = []
    for j in range(heads * per):
        part = video[:, j * block : (j + 1) * block]
        chunk_sets.append([part] + [shift(part, "heads", r) for r in ring])

    anywhere = pl.BlockSpec(memory_space=pl.ANY)
    sources = [spatial_out, temporal_qkv, temporal_out]
    mine_out, mine_time, mine_last = pl.pallas_call(
        functools.partial(pick_kernel, groups, cfg),
        out_shape=(
            jax.ShapeDtypeStruct((rows, D), jnp.bfloat16),
            jax.ShapeDtypeStruct((3, rows, D), jnp.bfloat16),
            jax.ShapeDtypeStruct((rows, D), jnp.bfloat16),
        ),
        in_specs=[anywhere] * 3,
        out_specs=(pl.BlockSpec(memory_space=pltpu.VMEM),) * 3,
        scratch_shapes=[pltpu.SemaphoreType.DMA((3,))],
        compiler_params=pltpu.CompilerParams(vmem_limit_bytes=8 << 20),
    )(*sources)

    chunks = []
    for j, chunk in enumerate(chunk_sets):
        if j == 0:
            text_kv, made = project_call(
                info, [text_set, chunk], [(1, 2), (0, 1, 2)], gain, spatial_qkv
            )
        else:
            ready = [chunk[0]] + [after(x, chunks[-1]) for x in chunk[1:]]
            (made,) = project_call(info, [ready], [(0, 1, 2)], gain, spatial_qkv)
        chunks.append(made)

    keys = [(r, dg, dc) for r in ring for dg in range(groups) for dc in range(cfg)]

    def first_hop(mine, gate):
        mine = after(mine, gate)
        return {(r, 0, 0): shift(mine, "heads", r) for r in ring}

    def second_hop(held, gate):
        for r in ring:
            for dg in range(1, groups):
                source = after(held[r, 0, 0], gate)
                held[r, dg, 0] = shift(source, "groups", dg)

    def third_hop(held, gate):
        for r in ring:
            for dg in range(groups):
                for dc in range(1, cfg):
                    source = after(held[r, dg, 0], gate)
                    held[r, dg, dc] = shift(source, "cfg", dc)

    arrived = chunk_sets[-1][-1]
    far_out = first_hop(mine_out, arrived)
    far_time = [first_hop(mine_time[0], arrived)]

    att = {}
    for r in ring:
        att[r] = attend_call(info, chunks, text_kv, heads, r)
    mark = att[heads - 1]
    for r in ring:
        att[r] = shift(att[r], "heads", r)
    far_time.append(first_hop(mine_time[1], mark))
    second_hop(far_out, mark)
    second_hop(far_time[0], mark)
    att[0] = attend_call(info, chunks, text_kv, heads, 0)
    third_hop(far_out, att[0])
    att_all = [att[r] for r in range(heads)]

    def held_tokens(r):
        return [x[r] for x in chunk_sets]

    split = (groups, cfg)
    near = out_call(
        info, att_all, [held_tokens(0)], [spatial_out], per, 16, seq, width, [(0, 0, 0)], split
    )
    far = out_call(
        info,
        att_all,
        [held_tokens(key[0]) for key in keys],
        [far_out[key] for key in keys],
        per,
        0,
        seq,
        D - width,
        keys,
        split,
    )
    far_time.append(first_hop(mine_time[2], near[0]))
    far_last = first_hop(mine_last, near[0])
    third_hop(far_time[0], far[0])
    second_hop(far_time[1], far[0])
    third_hop(far_time[1], far[0])
    second_hop(far_time[2], far[0])
    second_hop(far_last, far[0])
    third_hop(far_time[2], far[0])
    third_hop(far_last, far[0])
    near = [near[0]] + [shift(near[k], "seq", k) for k in range(1, seq)]
    far = [far[0]] + [shift(far[k], "seq", k) for k in range(1, seq)]

    keep, send, ratios = time_call(
        info,
        near,
        far,
        gain,
        temporal_qkv,
        temporal_out,
        [far_time[kind][key] for key in keys for kind in range(3)],
        [far_last[key] for key in keys],
        heads,
        groups,
        cfg,
        keys,
    )
    other = shift(send, "cfg", 1)
    slot = D // (heads * cfg)
    pieces = resident(
        guide_kernel,
        [((slot, lanes), jnp.bfloat16)] * (seq * heads),
        info,
        [keep, other, ratios],
        [],
        seq * D * lanes,
        8,
    )
    landed = []
    for k in range(seq):
        for r in range(heads):
            piece = pieces[k * heads + r]
            if k or r:
                route = [
                    (a * heads + b, (a - k) % seq * heads + (b + r) % heads)
                    for a in range(seq)
                    for b in range(heads)
                ]
                piece = lax.ppermute(piece, ("seq", "heads"), route)
            landed.append(piece)
    (result,) = resident(
        functools.partial(place_kernel, seq, heads),
        [((slot, positions), jnp.bfloat16)],
        info,
        landed,
        [],
        0,
        8,
        out_local=False,
    )
    return result[None]


def solution(mesh):
    return jax.shard_map(
        functools.partial(shards, fits(mesh)),
        mesh=mesh,
        in_specs=(
            P("cfg", ("groups", "seq"), "heads", None),
            P("cfg", ("groups", "seq"), "heads", None),
            P("cfg", ("groups", "seq")),
            P(("groups", "seq")),
            P(("groups", "seq")),
            P(),
            P(None, "heads", None),
            P("heads", None),
            P(),
            P(None, "heads", None),
            P("heads", None),
        ),
        out_specs=P(("groups", "seq"), ("heads", "cfg"), None),
        check_vma=False,
    )
```

```python
import functools

import jax
import jax.numpy as jnp
from jax import lax
from jax.experimental import pallas as pl
from jax.experimental.pallas import tpu as pltpu
from jax.sharding import PartitionSpec as P

D = 1152
HEAD_DIM = 72
HEAD_ROWS = 80
LANES = 128
HEADS, SEQ, GROUPS, CFG = "heads", "seq", "groups", "cfg"


epsilon = 1e-06


def from_partner(shard, axis, stride):
    return lax.ppermute(shard, axis, [(i, i ^ 1 << stride) for i in range(lax.axis_size(axis))])


def softmax_along(scores, axis):
    top_score = jnp.max(scores, axis=axis, keepdims=True)
    expons = jnp.exp(scores - top_score)
    return (expons / jnp.sum(expons, axis=axis, keepdims=True)).astype(jnp.bfloat16)


def project_piece(piece, gain_vector, weights, parts):
    gain_piece = gain_vector.astype(jnp.float32)
    weight_piece = weights[parts]
    piece_wide = piece.astype(jnp.float32)
    scaled = (piece_wide * gain_piece[None, :, None]).astype(jnp.bfloat16)
    product = jnp.einsum("kod,fdp->fkop", weight_piece, scaled, preferred_element_type=jnp.float32)
    return (product, jnp.sum(piece_wide * piece_wide, axis=1))


def add_mixed(piece, matrix):
    return jnp.einsum("oc,fcp->fop", matrix, piece, preferred_element_type=jnp.float32)


def shards_plain(
    video_tokens,
    text_tokens,
    text_length,
    guide_numer,
    guide_denom,
    spatial_gain,
    spatial_qkv,
    spatial_out,
    temporal_gain,
    temporal_qkv,
    temporal_out,
):
    frame_count = video_tokens.shape[1]
    width = video_tokens.shape[2]
    positions = video_tokens.shape[3]
    text_count = text_tokens.shape[3]
    local_heads = width // HEAD_DIM
    frame_tokens = video_tokens[0]
    frame_text = text_tokens[0]
    video_piece = lax.all_gather(frame_tokens, HEADS, axis=1, tiled=True)
    text_piece = lax.all_gather(frame_text, HEADS, axis=1, tiled=True)
    video_add, video_sq = project_piece(video_piece, spatial_gain, spatial_qkv, slice(0, 3))
    text_add, text_sq = project_piece(text_piece, spatial_gain, spatial_qkv, slice(1, 3))
    mixed = (video_add * lax.rsqrt(video_sq / D + epsilon)[:, None, None, :]).astype(jnp.bfloat16)
    mixed = mixed.reshape(frame_count, 3, local_heads, HEAD_DIM, positions)
    context = (text_add * lax.rsqrt(text_sq / D + epsilon)[:, None, None, :]).astype(jnp.bfloat16)
    context = context.reshape(frame_count, 2, local_heads, HEAD_DIM, text_count)
    key_rows = jnp.concatenate([mixed[:, 1], context[:, 0]], axis=3)
    value_rows = jnp.concatenate([mixed[:, 2], context[:, 1]], axis=3)
    query_all = mixed[:, 0]
    text_valid = jnp.arange(text_count, dtype=jnp.int32)[None, :] < text_length[0][:, None]
    valid_keys = jnp.concatenate(
        [jnp.ones((frame_count, positions), dtype=bool), text_valid], axis=1
    )
    block_rows = min(512, positions)
    block_count = positions // block_rows
    frame_ids = jnp.repeat(jnp.arange(frame_count, dtype=jnp.int32), block_count)
    block_ids = jnp.tile(jnp.arange(block_count, dtype=jnp.int32), frame_count)

    def block_step(inputs):
        frame_id, block_id = inputs
        query_rows = lax.dynamic_slice_in_dim(
            query_all[frame_id], block_id * block_rows, block_rows, 2
        )
        scores = jnp.einsum(
            "hep,hek->hpk", query_rows, key_rows[frame_id], preferred_element_type=jnp.float32
        )
        scores = scores * HEAD_DIM ** (-0.5)
        scores = jnp.where(valid_keys[frame_id][None, None, :], scores, -jnp.inf)
        weights = softmax_along(scores, 2)
        result = jnp.einsum(
            "hpk,hek->hep", weights, value_rows[frame_id], preferred_element_type=jnp.float32
        )
        return result.astype(jnp.bfloat16)

    attended = lax.map(block_step, (frame_ids, block_ids))
    attended = attended.reshape(frame_count, block_count, local_heads, HEAD_DIM, block_rows)
    attended = jnp.transpose(attended, (0, 2, 3, 1, 4)).reshape(frame_count, width, positions)
    update = add_mixed(lax.all_gather(attended, HEADS, axis=1, tiled=True), spatial_out)
    after_spatial = (frame_tokens.astype(jnp.float32) + update).astype(jnp.bfloat16)
    own_rows = lax.all_to_all(after_spatial, SEQ, split_axis=2, concat_axis=0, tiled=True)
    frames_all = own_rows.shape[0]
    columns = own_rows.shape[2]
    piece_add, piece_sq = project_piece(
        lax.all_gather(own_rows, HEADS, axis=1, tiled=True),
        temporal_gain,
        temporal_qkv,
        slice(0, 3),
    )
    mixed_time = (piece_add * lax.rsqrt(piece_sq / D + epsilon)[:, None, None, :]).astype(
        jnp.bfloat16
    )
    mixed_time = mixed_time.reshape(frames_all, 3, local_heads, HEAD_DIM, columns)
    time_scores = jnp.einsum(
        "fhep,ghep->hfgp", mixed_time[:, 0], mixed_time[:, 1], preferred_element_type=jnp.float32
    )
    time_weights = softmax_along(time_scores * HEAD_DIM ** (-0.5), 2)
    attended_time = jnp.einsum(
        "hfgp,ghep->fhep", time_weights, mixed_time[:, 2], preferred_element_type=jnp.float32
    )
    attended_time = attended_time.astype(jnp.bfloat16).reshape(frames_all, width, columns)
    update_time = add_mixed(
        lax.all_gather(attended_time, HEADS, axis=1, tiled=True), temporal_out
    )
    block_out = (own_rows.astype(jnp.float32) + update_time).astype(jnp.bfloat16)
    returned = lax.all_to_all(block_out, SEQ, split_axis=0, concat_axis=2, tiled=True)
    half_width = width // 2
    partner = from_partner(returned, CFG, 0)
    branch_index = lax.axis_index(CFG)
    cond_full = jnp.where(branch_index == 0, returned, partner)
    uncond_full = jnp.where(branch_index == 0, partner, returned)
    cond_part = lax.dynamic_slice_in_dim(cond_full, branch_index * half_width, half_width, 1)
    uncond_part = lax.dynamic_slice_in_dim(uncond_full, branch_index * half_width, half_width, 1)
    ratio = guide_numer.astype(jnp.float32) / guide_denom.astype(jnp.float32)
    cond_wide = cond_part.astype(jnp.float32)
    uncond_wide = uncond_part.astype(jnp.float32)
    return (uncond_wide + ratio[:, None, None] * (cond_wide - uncond_wide)).astype(jnp.bfloat16)


def fits(mesh):
    heads = mesh.shape[HEADS]
    share = mesh.shape[GROUPS] * mesh.shape[CFG]
    return (D // (heads * share)) % (2 * HEAD_DIM) == 0


def aligned(offset, step=16):
    return pl.multiple_of(offset, step)


def local(x):
    return pltpu.with_memory_space_constraint(x, pltpu.VMEM)


def resident(kernel, shapes, info, operands, scratch, flops, grant, exps=0, out_local=True):
    place = pl.BlockSpec(memory_space=pltpu.VMEM)
    kind = pltpu.VMEM if out_local else jax.ShapeDtypeStruct
    moved = sum(x.size * x.dtype.itemsize for x in operands)
    return pl.pallas_call(
        kernel,
        out_shape=tuple(kind(shape, dtype) for shape, dtype in shapes),
        in_specs=[pl.BlockSpec(memory_space=pltpu.SMEM)] + [place] * len(operands),
        out_specs=(place,) * len(shapes),
        scratch_shapes=scratch,
        compiler_params=pltpu.CompilerParams(vmem_limit_bytes=grant << 20),
        cost_estimate=pl.CostEstimate(flops=flops, bytes_accessed=moved, transcendentals=exps),
    )(info, *[local(x) for x in operands])


def place_of(axis):
    return lax.axis_index(axis)


def base_of(heads, r, width):
    return lax.rem(place_of(HEADS) - r + heads, heads) * width


def quarter_of(block, rows, groups, cfg):
    _, dg, dc = block
    g = lax.rem(place_of(GROUPS) - dg + groups, groups)
    return (g * cfg + lax.rem(place_of(CFG) - dc + cfg, cfg)) * rows


def weave(y, inverse, tail):
    heads = y.shape[0] // HEAD_DIM
    y = (y * inverse).reshape(heads, HEAD_DIM, y.shape[1])
    return jnp.concatenate([y, jnp.broadcast_to(tail, (heads,) + tail.shape)], axis=1)


def project_kernel(parts, jobs, info, *refs):
    inputs, refs = refs[: parts * len(jobs)], refs[parts * len(jobs) :]
    gain, w, refs = refs[0], refs[1], refs[2:]
    outs, scaled_refs = refs[: len(jobs)], refs[len(jobs) :]
    width = w.shape[1]
    for i, kinds in enumerate(jobs):
        scaled, total = scaled_refs[i], None
        for r in range(parts):
            rows = pl.ds(aligned(base_of(parts, r, width)), width)
            wide = inputs[i * parts + r][...].astype(jnp.float32)
            scaled[rows, :] = (wide * gain[rows, :]).astype(jnp.bfloat16)
            sq = jnp.sum(wide * wide, axis=0, keepdims=True)
            total = sq if total is None else total + sq
        inverse = lax.rsqrt(total / D + epsilon)
        row = lax.broadcasted_iota(
            jnp.int32, (HEAD_ROWS - HEAD_DIM, scaled.shape[1]), 0
        )
        for slot, kind in enumerate(kinds):
            y = jnp.dot(w[kind], scaled[...], preferred_element_type=jnp.float32)
            tail = jnp.where((row == 0) & (kind == 2), 1.0, 0.0)
            rate = HEAD_DIM ** (-0.5) * 1.4426950408889634 if kind == 0 else 1.0
            outs[i][slot] = weave(y, inverse * rate, tail).astype(jnp.bfloat16)


def project_call(info, sets, jobs, gain, w):
    width = w.shape[1]
    heads = width // HEAD_DIM
    parts = len(sets[0])
    counts = [x[0].shape[1] for x in sets]
    shapes = [
        ((len(kinds), heads, HEAD_ROWS, n), jnp.bfloat16) for kinds, n in zip(jobs, counts)
    ]
    return resident(
        functools.partial(project_kernel, parts, jobs),
        shapes,
        info,
        [x for group in sets for x in group] + [gain, w],
        [pltpu.VMEM((D, n), jnp.bfloat16) for n in counts],
        6 * width * D * sum(counts),
        12,
    )


def crossing(seq, cross):
    half = lax.div(place_of(SEQ), seq // 2)
    return 1 - half if cross else half


def pick_chunk(chunks, index, read):
    value = read(chunks[0])
    for i in range(1, len(chunks)):
        value = jnp.where(index == i, read(chunks[i]), value)
    return value


def attend_kernel(parts, aheads, count, with_text, resumed, final, info, *refs):
    queries, refs = refs[:parts], refs[parts:]
    keys, refs = list(refs[:count]), refs[count:]
    text = None
    if with_text:
        text, refs = refs[0], refs[1:]
    states, refs = refs[: 2 * len(aheads) * resumed], refs[2 * len(aheads) * resumed :]
    outs, (s_buf, m_buf, *o_buf) = refs[: len(aheads) * (2 - final)], refs[len(aheads) * (2 - final) :]
    heads, block = keys[0].shape[1], keys[0].shape[3]
    contract = (((0,), (0,)), ((), ()))

    def fold(s):
        return jnp.max(s.reshape(s.shape[0] // 8, 8, s.shape[1]), axis=0)

    group = s_buf.shape[1] // len(aheads)
    items = [(n, u) for n in range(len(aheads)) for u in range(group)]

    def score(stage, slot):
        for j, (n, u) in enumerate(items):
            head = stage * group + u
            index = lax.rem(place_of(HEADS) + aheads[n], parts)
            q = pick_chunk(queries, index, lambda chunk: chunk[0, head])
            top = None
            for i, chunk in enumerate(keys):
                s = lax.dot_general(
                    chunk[1, head], q, contract, preferred_element_type=jnp.float32
                )
                s_buf[slot, j, i * block : (i + 1) * block, :] = s
                top = fold(s) if top is None else jnp.maximum(top, fold(s))
            if with_text:
                t = lax.dot_general(
                    text[0, head], q, contract, preferred_element_type=jnp.float32
                )
                live = lax.broadcasted_iota(jnp.int32, t.shape, 0) < info[0]
                t = jnp.where(live, t, -jnp.inf)
                s_buf[slot, j, count * block :, :] = t
                top = jnp.maximum(top, fold(t))
            m_buf[slot, j] = top

    def mix(stage, slot):
        for j, (n, u) in enumerate(items):
            head = stage * group + u
            top = jnp.max(m_buf[slot, j], axis=0, keepdims=True)
            o = None
            if resumed:
                before = states[2 * n + 1][head, 0:1, :]
                top = jnp.maximum(top, before)
                o = states[2 * n][head] * jnp.exp2(before - top)
            for i in range(count + with_text):
                if i < count:
                    s, v = s_buf[slot, j, i * block : (i + 1) * block, :], keys[i][2, head]
                else:
                    s, v = s_buf[slot, j, count * block :, :], text[1, head]
                e = jnp.exp2(s - top).astype(jnp.bfloat16)
                term = jnp.dot(v, e, preferred_element_type=jnp.float32)
                o = term if o is None else o + term
            if final:
                rows = pl.ds(aligned(head * HEAD_DIM, 8), HEAD_DIM)
                o_buf[n][rows, :] = o[:HEAD_DIM] / o[HEAD_DIM : HEAD_DIM + 1]
            else:
                outs[2 * n][head] = o
                outs[2 * n + 1][head] = jnp.broadcast_to(top, (8, block))

    stages = heads // group
    score(0, 0)

    def step(i, carry):
        score(2 * i + 1, 1)
        mix(2 * i, 0)
        score(2 * i + 2, 0)
        mix(2 * i + 1, 1)
        return carry

    lax.fori_loop(0, stages // 2 - 1, step, 0)
    score(stages - 1, 1)
    mix(stages - 2, 0)
    mix(stages - 1, 1)
    if final:
        for n in range(len(aheads)):
            outs[n][...] = o_buf[n][...].astype(jnp.bfloat16)


def attend_call(info, queries, keys, text, states, aheads, final):
    parts, count = len(queries), len(keys)
    _, heads, _, block = keys[0].shape
    rows = block * count + (text.shape[3] if text is not None else 0)
    items = len(aheads) * (2 if count == 1 and heads % 4 == 0 else 1)
    if final:
        shapes = [((heads * HEAD_DIM, block), jnp.bfloat16)] * len(aheads)
        extra = [pltpu.VMEM((heads * HEAD_DIM, block), jnp.float32)] * len(aheads)
    else:
        shapes = [
            ((heads, HEAD_ROWS, block), jnp.float32),
            ((heads, 8, block), jnp.float32),
        ] * len(aheads)
        extra = []
    return resident(
        functools.partial(
            attend_kernel,
            parts,
            aheads,
            count,
            int(text is not None),
            int(bool(states)),
            int(final),
        ),
        shapes,
        info,
        list(queries) + list(keys) + ([text] if text is not None else []) + list(states),
        [
            pltpu.VMEM((2, items, rows, block), jnp.float32),
            pltpu.VMEM((2, items, 8, block), jnp.float32),
        ]
        + extra,
        4 * heads * 256 * block * rows * len(aheads),
        12,
        heads * block * rows * len(aheads),
    )


def out_kernel(n, extra, seq, blocks, share, info, *refs):
    att, refs = refs[:n], refs[n:]
    tokens, refs = refs[: n * len(blocks)], refs[n * len(blocks) :]
    w, refs = refs[: len(blocks)], refs[len(blocks) :]
    outs, (a, held) = refs[:-2], refs[-2:]
    width = att[0].shape[0]
    lanes = outs[0].shape[1]
    index = place_of(HEADS)
    skip = 0 if extra else width
    for r in range(n):
        a[pl.ds(aligned(base_of(n, r, width)), width), :] = att[r][...]
    far_w = [w[b][...] for b, key in enumerate(blocks) if key[0]]
    if far_w:
        far_y = jnp.dot(
            jnp.concatenate(far_w, axis=0), a[...], preferred_element_type=jnp.float32
        )
    done = 0
    for b, key in enumerate(blocks):
        count = w[b].shape[0]
        if key[0]:
            y = far_y[done : done + count]
            done += count
            offset = aligned(quarter_of(key, count, *share))
            inner, rows = pl.ds(offset, count), pl.ds(aligned(key[0] * width - skip + offset), count)
        else:
            y = jnp.dot(w[b][...], a[...], preferred_element_type=jnp.float32)
            inner, rows = slice(0, width), slice(0, width)
        x = pick_chunk(tokens[b * n : (b + 1) * n], index, lambda t: t[inner, :])
        held[rows, :] = (x.astype(jnp.float32) + y).astype(jnp.bfloat16)
    row = lax.broadcasted_iota(jnp.int32, (16, lanes), 0)
    numer, denom = info[1].astype(jnp.float32), info[2].astype(jnp.float32)
    tail = jnp.where(row == 0, numer, jnp.where(row == 1, denom, 0.0)).astype(jnp.bfloat16)
    outs = list(outs)
    for start, stop in [(0, width)] * bool(extra) + [(width, D)] * (held.shape[0] > width or not extra):
        for m in range(seq // 2):
            out = outs.pop(0)
            dest = lax.rem(lax.rem(place_of(SEQ), seq // 2) + m, seq // 2)
            span = pl.ds(aligned(dest * lanes, LANES), lanes)
            out[0 : stop - start, :] = held[start - skip : stop - skip, span]
            if start == 0:
                out[stop:, :] = tail


def out_call(info, att, tokens, w, extra, seq, blocks, share):
    n = len(att)
    width, count = att[0].shape
    total = sum(x.shape[0] for x in w)
    own = [((width + extra, 2 * count // seq), jnp.bfloat16)] * (seq // 2)
    other = [((D - width, 2 * count // seq), jnp.bfloat16)] * (seq // 2)
    return resident(
        functools.partial(out_kernel, n, extra, seq, blocks, share),
        own * bool(extra) + other * (total > width or not extra),
        info,
        list(att) + [x for group in tokens for x in group] + list(w),
        [pltpu.VMEM((D, count), jnp.bfloat16), pltpu.VMEM((total, count), jnp.bfloat16)],
        2 * D * total * count,
        12,
    )


def time_attend(read, att, rows, frames, heads):
    query, key, value = [
        [read(kind, f).reshape(heads, HEAD_DIM, read(kind, f).shape[1]) for f in range(frames)]
        for kind in range(3)
    ]
    lanes = query[0].shape[2]
    for f in range(frames):
        scores = [
            jnp.sum(query[f] * key[g], axis=1, keepdims=True) * HEAD_DIM ** (-0.5)
            for g in range(frames)
        ]
        top = functools.reduce(jnp.maximum, scores)
        expons = [jnp.exp(x - top) for x in scores]
        bottom = functools.reduce(jnp.add, expons)
        result = None
        for g in range(frames):
            weight = (expons[g] / bottom).astype(jnp.bfloat16).astype(jnp.float32)
            term = weight * value[g]
            result = term if result is None else result + term
        att[rows, f * lanes : (f + 1) * lanes] = result.reshape(
            heads * HEAD_DIM, lanes
        ).astype(jnp.bfloat16)


def time_project(near, far, gain, w, xs, inverse, out, parts, done=None):
    lanes = near[0].shape[1]
    width = w.shape[1]
    for f in range(len(near)):
        cols = slice(f * lanes, (f + 1) * lanes)
        total = None
        for r in range(parts):
            base = base_of(parts, r, width)
            if r == 0:
                x = near[f][0:width, :]
            else:
                x = far[f][(r - 1) * width : r * width, :]
            x = x.astype(jnp.float32)
            xs[pl.ds(aligned(base), width), cols] = (
                x * gain[pl.ds(aligned(D + base), width), :]
            ).astype(jnp.bfloat16)
            sq = jnp.sum(x * x, axis=0, keepdims=True)
            total = sq if total is None else total + sq
        inverse[:, cols] = jnp.broadcast_to(lax.rsqrt(total / D + epsilon), (8, lanes))
    for top in range(0, width, width // 2):
        span = slice(top, top + width // 2)
        for kind in range(3):
            y = jnp.dot(w[kind, span, :], xs[...], preferred_element_type=jnp.float32)
            out[kind, span, :] = (y * inverse[0:1, :]).astype(jnp.bfloat16)
        if done is not None:
            done(span)


def time_cross_kernel(frames, parts, info, *refs):
    near, far, refs = refs[:frames], refs[frames : 2 * frames], refs[2 * frames :]
    gain, w, xs, inverse, out = refs
    time_project(near, far, gain, w, xs, inverse, out, parts)


def time_near_kernel(frames, parts, share, info, *refs):
    near, far, refs = refs[:frames], refs[frames : 2 * frames], refs[2 * frames :]
    gain, w, crossed, xs, inverse, att, out = refs
    lanes = near[0].shape[1]
    rows = w.shape[1] // share

    def attend(part):
        for top in range(part.start, part.stop, rows):
            span = slice(top, top + rows)

            def read(kind, f):
                source = out if f < frames else crossed
                start = f % frames * lanes
                return source[kind, span, start : start + lanes].astype(jnp.float32)

            time_attend(read, att, span, 2 * frames, rows // HEAD_DIM)

    time_project(near, far, gain, w, xs, inverse, out, parts, attend)


def time_far_kernel(frames, share, keys, width, info, *refs):
    sides, refs = (refs[0:2], refs[2:4]), refs[4:]
    w, att = refs[:-1], refs[-1]
    rows = w[0].shape[0]
    half = frames // 2
    lanes = att.shape[1] // frames
    for b, key in enumerate(keys):
        span = pl.ds(aligned((key[0] - 1) * width + quarter_of(key, rows, *share)), rows)
        made = []
        for kind in range(3):
            part = w[2 * b][...] if kind == 0 else w[2 * b + 1][(kind - 1) * rows : kind * rows, :]
            for xs, inverse in sides:
                y = jnp.dot(part, xs[...], preferred_element_type=jnp.float32)
                made.append((y * inverse[0:1, :]).astype(jnp.bfloat16).astype(jnp.float32))

        def read(kind, f):
            start = f % half * lanes
            return made[2 * kind + f // half][:, start : start + lanes]

        time_attend(read, att, span, frames, rows // HEAD_DIM)


def time_cross_call(info, near, far, gain, w, parts):
    frames, lanes = len(near), near[0].shape[1]
    width, count = w.shape[1], frames * lanes
    return resident(
        functools.partial(time_cross_kernel, frames, parts),
        [
            ((D, count), jnp.bfloat16),
            ((8, count), jnp.float32),
            ((3, width, count), jnp.bfloat16),
        ],
        info,
        list(near) + list(far) + [gain, w],
        [],
        6 * D * width * count,
        12,
    )


def time_near_call(info, near, far, gain, w, crossed, parts, share):
    frames, lanes = len(near), near[0].shape[1]
    width, count = w.shape[1], frames * lanes
    return resident(
        functools.partial(time_near_kernel, frames, parts, share),
        [
            ((D, count), jnp.bfloat16),
            ((8, count), jnp.float32),
            ((width, 2 * count), jnp.bfloat16),
        ],
        info,
        list(near) + list(far) + [gain, w, crossed],
        [pltpu.VMEM((3, width, count), jnp.bfloat16)],
        6 * D * width * count,
        12,
    )


def time_far_call(info, sides, w, frames, share, keys, width):
    count = 2 * sides[0].shape[1]
    return resident(
        functools.partial(time_far_kernel, frames, share, keys, width),
        [((D - width, count), jnp.bfloat16)],
        info,
        list(sides) + list(w),
        [],
        6 * D * (D - width) * count,
        12,
    )[0]


def time_out_kernel(frames, parts, share, keys, first, info, *refs):
    near, refs = refs[:frames], refs[frames:]
    far, refs = refs[:frames], refs[frames:]
    att_near, att_far, o_own, refs = refs[0], refs[1], refs[2], refs[3:]
    o_far, (keep, send, ratios, att, res) = refs[: len(keys)], refs[len(keys) :]
    lanes = near[0].shape[1]
    width = o_own.shape[0]
    head_index, branch = place_of(HEADS), place_of(CFG)
    for r in range(parts):
        span = pl.ds(aligned(base_of(parts, r, width)), width)
        cols = slice(first * lanes, (first + frames) * lanes)
        att[span, :] = (
            att_near[:, cols] if r == 0 else att_far[(r - 1) * width : r * width, cols]
        )
    far_y = jnp.dot(
        jnp.concatenate([x[...] for x in o_far], axis=0),
        att[...],
        preferred_element_type=jnp.float32,
    )
    done = 0
    for key in [(0, 0, 0)] + list(keys):
        base = base_of(parts, key[0], width)
        if key[0]:
            count = o_far[keys.index(key)].shape[0]
            offset = quarter_of(key, count, *share)
            source, start = far, (key[0] - 1) * width + offset
            y = far_y[done : done + count]
            done += count
        else:
            count, offset, source, start = width, 0, near, 0
            y = jnp.dot(o_own[...], att[...], preferred_element_type=jnp.float32)
        for f in range(frames):
            if key[0]:
                x = source[f][pl.ds(aligned(start), count), :]
            else:
                x = source[f][0:count, :]
            x = x.astype(jnp.float32) + y[:, f * lanes : (f + 1) * lanes]
            res[f, pl.ds(aligned(base + offset), count), :] = x.astype(jnp.bfloat16)
    slot = keep.shape[2]
    for f in range(frames):
        tail = near[f][width:, :].astype(jnp.float32)
        ratios[f : f + 1, :] = tail[0:1] / tail[1:2]
        for r in range(parts):
            head = lax.rem(head_index + r, parts)
            keep[f, r] = res[f, pl.ds(aligned((head * 2 + branch) * slot), slot), :]
            send[f, r] = res[f, pl.ds(aligned((head * 2 + 1 - branch) * slot), slot), :]


def time_out_call(
    info, near, far, att_near, att_far, o_own, o_far, parts, share, keys, first
):
    frames, lanes = len(near), near[0].shape[1]
    result = ((frames, parts, D // (2 * parts), lanes), jnp.bfloat16)
    return resident(
        functools.partial(time_out_kernel, frames, parts, share, keys, first),
        [result, result, ((frames, lanes), jnp.float32)],
        info,
        list(near) + list(far) + [att_near, att_far, o_own] + list(o_far),
        [
            pltpu.VMEM((D, frames * lanes), jnp.bfloat16),
            pltpu.VMEM((frames, D, lanes), jnp.bfloat16),
        ],
        2 * D * D * frames * lanes,
        12,
    )


def guide_kernel(info, keep, other, ratios, *outs):
    frames, parts = keep.shape[0], keep.shape[1]
    branch = place_of(CFG)
    for f in range(frames):
        ratio = ratios[f : f + 1, :]
        for r in range(parts):
            mine = keep[f, r].astype(jnp.float32)
            theirs = other[f, r].astype(jnp.float32)
            cond = jnp.where(branch == 0, mine, theirs)
            uncond = jnp.where(branch == 0, theirs, mine)
            outs[f * parts + r][...] = (uncond + ratio * (cond - uncond)).astype(jnp.bfloat16)


def place_kernel(seq, parts, *refs):
    pieces, out, sems = refs[:-2], refs[-2], refs[-1]
    head, frame = place_of(HEADS), place_of(SEQ)
    half = seq // 2
    copies = []
    for i, (cross, m) in enumerate(roads(seq)):
        side = crossing(seq, cross) * half + lax.rem(lax.rem(frame, half) + m, half)
        for r in range(parts):
            piece = pieces[i * parts + r]
            slot = lax.rem(head - r + parts, parts) * seq + side
            lanes = piece.shape[1]
            view = out.at[:, pl.ds(aligned(slot * lanes, LANES), lanes)]
            copies.append(pltpu.make_async_copy(piece, view, sems.at[i * parts + r]))
    for copy in copies:
        copy.start()
    for copy in copies:
        copy.wait()


def place_call(pieces, seq, parts):
    rows, lanes = pieces[0].shape
    n = len(pieces)
    return pl.pallas_call(
        functools.partial(place_kernel, seq, parts),
        out_shape=jax.ShapeDtypeStruct((rows, n * lanes), jnp.bfloat16),
        in_specs=[pl.BlockSpec(memory_space=pltpu.VMEM)] * n,
        out_specs=pl.BlockSpec(memory_space=pltpu.HBM),
        scratch_shapes=[pltpu.SemaphoreType.DMA((n,))],
        compiler_params=pltpu.CompilerParams(vmem_limit_bytes=4 << 20),
    )(*[local(x) for x in pieces])


def split_kernel(seq, parts, source, *refs):
    outs, sems = refs[:-1], refs[-1]
    copies = []
    for i, out in enumerate(outs):
        block = out.shape[1]
        start = ((i % parts) * 2 + crossing(seq, i < parts)) * block
        view = source.at[:, pl.ds(aligned(start, LANES), block)]
        copies.append(pltpu.make_async_copy(view, out, sems.at[i]))
    for copy in copies:
        copy.start()
    for copy in copies:
        copy.wait()


def pick_kernel(share, w_out, w_time, w_last, w_space, gains, *refs):
    outs, w_here, column, sems = refs[:-3], refs[-3], refs[-2], refs[-1]
    rows = outs[-1].shape[0]
    start = quarter_of((0, 0, 0), rows, *share)
    inner = start + lax.rem(place_of(SEQ), 2) * outs[0].shape[0]
    moves = [
        (w_out, inner, outs[0]),
        (w_time.at[0], inner, outs[1]),
        (w_time.at[1], start, outs[2].at[0:rows, :]),
        (w_time.at[2], start, outs[2].at[rows:, :]),
        (w_last, start, outs[3]),
        (w_space, None, w_here),
    ]
    copies = []
    for i, (source, first, out) in enumerate(moves):
        view = source if first is None else source.at[pl.ds(aligned(first, 8), out.shape[0]), :]
        copies.append(pltpu.make_async_copy(view, out, sems.at[i]))
    for copy in copies:
        copy.start()
    row = lax.broadcasted_iota(jnp.int32, (LANES, LANES), 0)
    diagonal = row == lax.broadcasted_iota(jnp.int32, (LANES, LANES), 1)
    for i in range(gains.shape[0]):
        wide = jnp.broadcast_to(gains[i : i + 1, :].astype(jnp.float32), (LANES, LANES))
        column[i * LANES : (i + 1) * LANES, :] = jnp.sum(
            jnp.where(diagonal, wide, 0.0), axis=1, keepdims=True
        )
    for copy in copies:
        copy.wait()


def stack_kernel(own, other, out, sems):
    rows = own.shape[0]
    side = lax.rem(place_of(SEQ), 2)
    copies = [
        pltpu.make_async_copy(own, out.at[pl.ds(aligned(side * rows, 8), rows), :], sems.at[0]),
        pltpu.make_async_copy(
            other, out.at[pl.ds(aligned((1 - side) * rows, 8), rows), :], sems.at[1]
        ),
    ]
    for copy in copies:
        copy.start()
    for copy in copies:
        copy.wait()


def stack_call(own, other):
    rows, columns = own.shape
    place = pl.BlockSpec(memory_space=pltpu.VMEM)
    return pl.pallas_call(
        stack_kernel,
        out_shape=pltpu.VMEM((2 * rows, columns), own.dtype),
        in_specs=[place, place],
        out_specs=place,
        scratch_shapes=[pltpu.SemaphoreType.DMA((2,))],
        compiler_params=pltpu.CompilerParams(vmem_limit_bytes=2 << 20),
    )(local(own), local(other))


def roads(seq):
    return [(cross, m) for cross in (0, 1) for m in range(seq // 2)]


def follow(seq, road, i, back=False):
    cross, m = road
    half = seq // 2
    side = i // half
    return (1 - side if cross else side) * half + (i % half + (-m if back else m)) % half


def shift(x, axis, by):
    size = lax.axis_size(axis)
    return lax.ppermute(x, axis, [(i, (i + by) % size) for i in range(size)])


def after(x, *gates):
    return lax.optimization_barrier((x,) + gates)[0]


def shards(fit, *args):
    (video_tokens, _, _, _, _, _, _, _, _, _, _) = args
    heads, seq = lax.axis_size(HEADS), lax.axis_size(SEQ)
    positions = video_tokens.shape[3]
    lanes = positions // (heads * seq)
    if not fit or lanes % LANES or seq % 4 or video_tokens.shape[1] != 1:
        return shards_plain(*args)
    return shards_fast(*args)


def shards_fast(
    video_tokens,
    text_tokens,
    text_length,
    guide_numer,
    guide_denom,
    spatial_gain,
    spatial_qkv,
    spatial_out,
    temporal_gain,
    temporal_qkv,
    temporal_out,
):
    heads, seq = lax.axis_size(HEADS), lax.axis_size(SEQ)
    groups, cfg = lax.axis_size(GROUPS), lax.axis_size(CFG)
    positions = video_tokens.shape[3]
    lanes = positions // (heads * seq)
    video, text = video_tokens[0, 0], text_tokens[0, 0]
    width = video.shape[0]
    rows = width // (groups * cfg)
    per = 2
    block = positions // (heads * per)
    ring = range(1, heads)
    info = jnp.concatenate([text_length[0], guide_numer, guide_denom])
    gains = jnp.concatenate([spatial_gain, temporal_gain]).reshape(-1, LANES)

    text_set = [text] + [shift(text, HEADS, r) for r in ring]
    parts = pl.pallas_call(
        functools.partial(split_kernel, seq, heads),
        out_shape=(jax.ShapeDtypeStruct((width, block), jnp.bfloat16),) * (heads * per),
        in_specs=[pl.BlockSpec(memory_space=pltpu.HBM)],
        out_specs=(pl.BlockSpec(memory_space=pltpu.VMEM),) * (heads * per),
        scratch_shapes=[pltpu.SemaphoreType.DMA((heads * per,))],
        compiler_params=pltpu.CompilerParams(vmem_limit_bytes=8 << 20),
    )(pltpu.with_memory_space_constraint(video, pltpu.HBM))
    chunk_sets = []
    for part in parts:
        chunk_sets.append([part] + [shift(part, HEADS, r) for r in ring])

    sources = [
        pltpu.with_memory_space_constraint(x, pltpu.HBM)
        for x in (spatial_out, temporal_qkv, temporal_out, spatial_qkv)
    ]
    whole, part = (rows, D), (rows // 2, D)
    *mine, spatial_here, gain = pl.pallas_call(
        functools.partial(pick_kernel, (groups, cfg)),
        out_shape=tuple(
            jax.ShapeDtypeStruct(shape, jnp.bfloat16)
            for shape in (part, part, (2 * rows, D), whole)
        )
        + (
            pltpu.VMEM(spatial_qkv.shape, jnp.bfloat16),
            pltpu.VMEM((2 * D, 1), jnp.float32),
        ),
        in_specs=[pl.BlockSpec(memory_space=pltpu.HBM)] * 4
        + [pl.BlockSpec(memory_space=pltpu.VMEM)],
        out_specs=(pl.BlockSpec(memory_space=pltpu.VMEM),) * 6,
        scratch_shapes=[pltpu.SemaphoreType.DMA((6,))],
        compiler_params=pltpu.CompilerParams(vmem_limit_bytes=12 << 20),
    )(*sources, gains)

    chunks = []
    mark, states = None, []
    aheads = list(range(1, heads)) + [0]
    for j, chunk in enumerate(chunk_sets):
        if j == 0:
            text_kv, made = project_call(
                info, [text_set, chunk], [(1, 2), (0, 1, 2)], gain, spatial_here
            )
        else:
            ready = [chunk[0]] + [after(x, mark) for x in chunk[1:]]
            (made,) = project_call(info, [ready], [(0, 1, 2)], gain, spatial_here)
        chunks.append(made)
        mark = made
        if heads - 1 <= j < heads * per - 1:
            fresh = chunks if j == heads - 1 else [made]
            states = attend_call(
                info,
                chunks[:heads],
                fresh,
                text_kv if j == heads - 1 else None,
                states,
                aheads,
                False,
            )
            mark = states[0]

    keys = [(r, dg, dc) for r in ring for dg in range(groups) for dc in range(cfg)]

    def first_hop(w, gate=None):
        w = w if gate is None else after(w, gate)
        return {(r, 0, 0): shift(w, HEADS, r) for r in ring}

    def trade(held, gate):
        pairs = [(i, i ^ 1) for i in range(seq)]
        for r in ring:
            own = after(held[r, 0, 0], gate)
            held[r, 0, 0] = own, lax.ppermute(own, SEQ, pairs)

    def join(held, gate):
        for r in ring:
            own, other = held[r, 0, 0]
            held[r, 0, 0] = stack_call(own, after(other, gate))

    def second_hop(held, gate):
        for r in ring:
            for dg in range(1, groups):
                source = after(held[r, 0, 0], gate)
                held[r, dg, 0] = shift(source, GROUPS, dg)

    def third_hop(held, gate):
        for r in ring:
            for dg in range(groups):
                for dc in range(1, cfg):
                    source = after(held[r, dg, 0], gate)
                    held[r, dg, dc] = shift(source, CFG, dc)

    far_out = first_hop(mine[0])
    far_time = [first_hop(mine[1])]
    att = {}

    def attend(cross, r):
        if cross:
            n = aheads.index(r)
            state = states[2 * n : 2 * n + 2]
            return attend_call(info, chunks[:heads], chunks[-1:], None, state, [r], True)[0]
        return attend_call(info, chunks[heads:], chunks, text_kv, [], [r], True)[0]

    def attend_far(cross):
        for r in ring:
            mark = attend(cross, r)
            att[cross, r] = shift(mark, HEADS, r)
        return mark

    def held_tokens(r, cross):
        return [x[r] for x in (chunk_sets[:heads] if cross else chunk_sets[heads:])]

    split = (groups, cfg)
    near, far = {}, {}

    def out_rows(cross, own, others):
        att_all = [att[cross, r] for r in range(heads)]
        part = [(0, 0, 0)] * own + keys * others
        got = out_call(
            info,
            att_all,
            [held_tokens(key[0], cross) for key in part],
            [far_out[key] if key[0] else spatial_out for key in part],
            16 * own,
            seq,
            part,
            split,
        )
        if own:
            near.update({(cross, m): got[m] for m in range(seq // 2)})
        if others:
            far.update({(cross, m): got[m + seq // 2 * own] for m in range(seq // 2)})
        return got[0]

    first = attend_far(1)
    trade(far_out, first)
    att[1, 0] = attend(1, 0)
    trade(far_time[0], att[1, 0])
    join(far_out, att[1, 0])
    second_hop(far_out, att[1, 0])
    early = out_rows(1, 1, 0)
    join(far_time[0], early)
    third_hop(far_out, early)
    second = attend_far(0)
    middle = out_rows(1, 0, 1)
    att[0, 0] = attend(0, 0)
    late = out_rows(0, 1, 1)
    far_time.append(first_hop(mine[2], first))
    far_last = first_hop(mine[3], second)
    for held, gate in zip(far_time, (early, second)):
        second_hop(held, gate)
        third_hop(held, late)

    def send_all(held):
        moved = []
        for road in roads(seq):
            x = held[road]
            if road != (0, 0):
                route = [(i, follow(seq, road, i)) for i in range(seq)]
                x = lax.ppermute(x, SEQ, route)
            moved.append(x)
        return moved

    near, far = send_all(near), send_all(far)
    second_hop(far_last, far[seq // 2])
    third_hop(far_last, far[seq // 2])
    share = groups * cfg
    mid = seq // 2
    xs_cross, inverse_cross, crossed = time_cross_call(
        info, near[mid:], far[mid:], gain, temporal_qkv, heads
    )
    xs, inverse, att_near = time_near_call(
        info, near[:mid], far[:mid], gain, temporal_qkv, crossed, heads, share
    )
    att_far = time_far_call(
        info,
        [xs, inverse, xs_cross, inverse_cross],
        [far_time[kind][key] for key in keys for kind in range(2)],
        seq,
        split,
        keys,
        width,
    )
    slot = D // (heads * cfg)
    landed = {}
    results = {}
    for cross in (1, 0):
        picked = [i for i, road in enumerate(roads(seq)) if road[0] == cross]
        keep, send, ratios = time_out_call(
            info,
            [near[i] for i in picked],
            [far[i] for i in picked],
            att_near,
            att_far,
            temporal_out,
            [far_last[key] for key in keys],
            heads,
            split,
            keys,
            picked[0],
        )
        results[cross] = keep, shift(send, CFG, 1), ratios
    for cross in (1, 0):
        picked = [i for i, road in enumerate(roads(seq)) if road[0] == cross]
        pieces = resident(
            guide_kernel,
            [((slot, lanes), jnp.bfloat16)] * (len(picked) * heads),
            info,
            results[cross],
            [],
            len(picked) * D * lanes,
            8,
        )
        for n, i in enumerate(picked):
            road = roads(seq)[i]
            for r in range(heads):
                piece = pieces[n * heads + r]
                if road != (0, 0) or r:
                    route = [
                        (a * heads + b, follow(seq, road, a, True) * heads + (b + r) % heads)
                        for a in range(seq)
                        for b in range(heads)
                    ]
                    piece = lax.ppermute(piece, (SEQ, HEADS), route)
                landed[i, r] = piece
    landed = [landed[i, r] for i in range(seq) for r in range(heads)]
    result = place_call(landed, seq, heads)
    return result[None]


def solution(mesh):
    return jax.shard_map(
        functools.partial(shards, fits(mesh)),
        mesh=mesh,
        in_specs=(
            P(CFG, (GROUPS, SEQ), HEADS, None),
            P(CFG, (GROUPS, SEQ), HEADS, None),
            P(CFG, (GROUPS, SEQ)),
            P((GROUPS, SEQ)),
            P((GROUPS, SEQ)),
            P(),
            P(None, HEADS, None),
            P(HEADS, None),
            P(),
            P(None, HEADS, None),
            P(HEADS, None),
        ),
        out_specs=P((GROUPS, SEQ), (HEADS, CFG), None),
        check_vma=False,
    )
```

```python
import functools

import jax
import jax.numpy as jnp
from jax import lax
from jax.experimental import pallas as pl
from jax.experimental.pallas import tpu as pltpu
from jax.sharding import PartitionSpec as P

D = 1152
HEAD_DIM = 72
HEAD_ROWS = 80
LANES = 128
HEADS, SEQ, GROUPS, CFG = "heads", "seq", "groups", "cfg"


epsilon = 1e-06


def from_partner(shard, axis, stride):
    return lax.ppermute(shard, axis, [(i, i ^ 1 << stride) for i in range(lax.axis_size(axis))])


def softmax_along(scores, axis):
    top_score = jnp.max(scores, axis=axis, keepdims=True)
    expons = jnp.exp(scores - top_score)
    return (expons / jnp.sum(expons, axis=axis, keepdims=True)).astype(jnp.bfloat16)


def project_piece(piece, gain_vector, weights, parts):
    gain_piece = gain_vector.astype(jnp.float32)
    weight_piece = weights[parts]
    piece_wide = piece.astype(jnp.float32)
    scaled = (piece_wide * gain_piece[None, :, None]).astype(jnp.bfloat16)
    product = jnp.einsum("kod,fdp->fkop", weight_piece, scaled, preferred_element_type=jnp.float32)
    return (product, jnp.sum(piece_wide * piece_wide, axis=1))


def add_mixed(piece, matrix):
    return jnp.einsum("oc,fcp->fop", matrix, piece, preferred_element_type=jnp.float32)


def shards_plain(
    video_tokens,
    text_tokens,
    text_length,
    guide_numer,
    guide_denom,
    spatial_gain,
    spatial_qkv,
    spatial_out,
    temporal_gain,
    temporal_qkv,
    temporal_out,
):
    frame_count = video_tokens.shape[1]
    width = video_tokens.shape[2]
    positions = video_tokens.shape[3]
    text_count = text_tokens.shape[3]
    local_heads = width // HEAD_DIM
    frame_tokens = video_tokens[0]
    frame_text = text_tokens[0]
    video_piece = lax.all_gather(frame_tokens, HEADS, axis=1, tiled=True)
    text_piece = lax.all_gather(frame_text, HEADS, axis=1, tiled=True)
    video_add, video_sq = project_piece(video_piece, spatial_gain, spatial_qkv, slice(0, 3))
    text_add, text_sq = project_piece(text_piece, spatial_gain, spatial_qkv, slice(1, 3))
    mixed = (video_add * lax.rsqrt(video_sq / D + epsilon)[:, None, None, :]).astype(jnp.bfloat16)
    mixed = mixed.reshape(frame_count, 3, local_heads, HEAD_DIM, positions)
    context = (text_add * lax.rsqrt(text_sq / D + epsilon)[:, None, None, :]).astype(jnp.bfloat16)
    context = context.reshape(frame_count, 2, local_heads, HEAD_DIM, text_count)
    key_rows = jnp.concatenate([mixed[:, 1], context[:, 0]], axis=3)
    value_rows = jnp.concatenate([mixed[:, 2], context[:, 1]], axis=3)
    query_all = mixed[:, 0]
    text_valid = jnp.arange(text_count, dtype=jnp.int32)[None, :] < text_length[0][:, None]
    valid_keys = jnp.concatenate(
        [jnp.ones((frame_count, positions), dtype=bool), text_valid], axis=1
    )
    block_rows = min(512, positions)
    block_count = positions // block_rows
    frame_ids = jnp.repeat(jnp.arange(frame_count, dtype=jnp.int32), block_count)
    block_ids = jnp.tile(jnp.arange(block_count, dtype=jnp.int32), frame_count)

    def block_step(inputs):
        frame_id, block_id = inputs
        query_rows = lax.dynamic_slice_in_dim(
            query_all[frame_id], block_id * block_rows, block_rows, 2
        )
        scores = jnp.einsum(
            "hep,hek->hpk", query_rows, key_rows[frame_id], preferred_element_type=jnp.float32
        )
        scores = scores * HEAD_DIM ** (-0.5)
        scores = jnp.where(valid_keys[frame_id][None, None, :], scores, -jnp.inf)
        weights = softmax_along(scores, 2)
        result = jnp.einsum(
            "hpk,hek->hep", weights, value_rows[frame_id], preferred_element_type=jnp.float32
        )
        return result.astype(jnp.bfloat16)

    attended = lax.map(block_step, (frame_ids, block_ids))
    attended = attended.reshape(frame_count, block_count, local_heads, HEAD_DIM, block_rows)
    attended = jnp.transpose(attended, (0, 2, 3, 1, 4)).reshape(frame_count, width, positions)
    update = add_mixed(lax.all_gather(attended, HEADS, axis=1, tiled=True), spatial_out)
    after_spatial = (frame_tokens.astype(jnp.float32) + update).astype(jnp.bfloat16)
    own_rows = lax.all_to_all(after_spatial, SEQ, split_axis=2, concat_axis=0, tiled=True)
    frames_all = own_rows.shape[0]
    columns = own_rows.shape[2]
    piece_add, piece_sq = project_piece(
        lax.all_gather(own_rows, HEADS, axis=1, tiled=True),
        temporal_gain,
        temporal_qkv,
        slice(0, 3),
    )
    mixed_time = (piece_add * lax.rsqrt(piece_sq / D + epsilon)[:, None, None, :]).astype(
        jnp.bfloat16
    )
    mixed_time = mixed_time.reshape(frames_all, 3, local_heads, HEAD_DIM, columns)
    time_scores = jnp.einsum(
        "fhep,ghep->hfgp", mixed_time[:, 0], mixed_time[:, 1], preferred_element_type=jnp.float32
    )
    time_weights = softmax_along(time_scores * HEAD_DIM ** (-0.5), 2)
    attended_time = jnp.einsum(
        "hfgp,ghep->fhep", time_weights, mixed_time[:, 2], preferred_element_type=jnp.float32
    )
    attended_time = attended_time.astype(jnp.bfloat16).reshape(frames_all, width, columns)
    update_time = add_mixed(
        lax.all_gather(attended_time, HEADS, axis=1, tiled=True), temporal_out
    )
    block_out = (own_rows.astype(jnp.float32) + update_time).astype(jnp.bfloat16)
    returned = lax.all_to_all(block_out, SEQ, split_axis=0, concat_axis=2, tiled=True)
    half_width = width // 2
    partner = from_partner(returned, CFG, 0)
    branch_index = lax.axis_index(CFG)
    cond_full = jnp.where(branch_index == 0, returned, partner)
    uncond_full = jnp.where(branch_index == 0, partner, returned)
    cond_part = lax.dynamic_slice_in_dim(cond_full, branch_index * half_width, half_width, 1)
    uncond_part = lax.dynamic_slice_in_dim(uncond_full, branch_index * half_width, half_width, 1)
    ratio = guide_numer.astype(jnp.float32) / guide_denom.astype(jnp.float32)
    cond_wide = cond_part.astype(jnp.float32)
    uncond_wide = uncond_part.astype(jnp.float32)
    return (uncond_wide + ratio[:, None, None] * (cond_wide - uncond_wide)).astype(jnp.bfloat16)


def fits(mesh):
    heads = mesh.shape[HEADS]
    share = mesh.shape[GROUPS] * mesh.shape[CFG]
    return (D // (heads * share)) % (2 * HEAD_DIM) == 0


def aligned(offset, step=16):
    return pl.multiple_of(offset, step)


def local(x):
    return pltpu.with_memory_space_constraint(x, pltpu.VMEM)


def resident(kernel, shapes, info, operands, scratch, flops, grant, exps=0, out_local=True):
    place = pl.BlockSpec(memory_space=pltpu.VMEM)
    kind = pltpu.VMEM if out_local else jax.ShapeDtypeStruct
    moved = sum(x.size * x.dtype.itemsize for x in operands)
    return pl.pallas_call(
        kernel,
        out_shape=tuple(kind(shape, dtype) for shape, dtype in shapes),
        in_specs=[pl.BlockSpec(memory_space=pltpu.SMEM)] + [place] * len(operands),
        out_specs=(place,) * len(shapes),
        scratch_shapes=scratch,
        compiler_params=pltpu.CompilerParams(vmem_limit_bytes=grant << 20),
        cost_estimate=pl.CostEstimate(flops=flops, bytes_accessed=moved, transcendentals=exps),
    )(info, *[local(x) for x in operands])


def place_of(axis):
    return lax.axis_index(axis)


def base_of(heads, r, width):
    return lax.rem(place_of(HEADS) - r + heads, heads) * width


def quarter_of(block, rows, groups, cfg):
    _, dg, dc = block
    g = lax.rem(place_of(GROUPS) - dg + groups, groups)
    return (g * cfg + lax.rem(place_of(CFG) - dc + cfg, cfg)) * rows


def weave(y, inverse, tail):
    heads = y.shape[0] // HEAD_DIM
    y = (y * inverse).reshape(heads, HEAD_DIM, y.shape[1])
    return jnp.concatenate([y, jnp.broadcast_to(tail, (heads,) + tail.shape)], axis=1)


def project_kernel(parts, jobs, info, *refs):
    inputs, refs = refs[: parts * len(jobs)], refs[parts * len(jobs) :]
    gain, w, refs = refs[0], refs[1], refs[2:]
    outs, scaled_refs = refs[: len(jobs)], refs[len(jobs) :]
    width = w.shape[1]
    for i, kinds in enumerate(jobs):
        scaled, total = scaled_refs[i], None
        for r in range(parts):
            rows = pl.ds(aligned(base_of(parts, r, width)), width)
            wide = inputs[i * parts + r][...].astype(jnp.float32)
            scaled[rows, :] = (wide * gain[rows, :]).astype(jnp.bfloat16)
            sq = jnp.sum(wide * wide, axis=0, keepdims=True)
            total = sq if total is None else total + sq
        inverse = lax.rsqrt(total / D + epsilon)
        row = lax.broadcasted_iota(
            jnp.int32, (HEAD_ROWS - HEAD_DIM, scaled.shape[1]), 0
        )
        for slot, kind in enumerate(kinds):
            y = jnp.dot(w[kind], scaled[...], preferred_element_type=jnp.float32)
            tail = jnp.where((row == 0) & (kind == 2), 1.0, 0.0)
            rate = HEAD_DIM ** (-0.5) * 1.4426950408889634 if kind == 0 else 1.0
            outs[i][slot] = weave(y, inverse * rate, tail).astype(jnp.bfloat16)


def project_call(info, sets, jobs, gain, w):
    width = w.shape[1]
    heads = width // HEAD_DIM
    parts = len(sets[0])
    counts = [x[0].shape[1] for x in sets]
    shapes = [
        ((len(kinds), heads, HEAD_ROWS, n), jnp.bfloat16) for kinds, n in zip(jobs, counts)
    ]
    return resident(
        functools.partial(project_kernel, parts, jobs),
        shapes,
        info,
        [x for group in sets for x in group] + [gain, w],
        [pltpu.VMEM((D, n), jnp.bfloat16) for n in counts],
        6 * width * D * sum(counts),
        12,
    )


def crossing(seq, cross):
    half = lax.div(place_of(SEQ), seq // 2)
    return 1 - half if cross else half


def pick_chunk(chunks, index, read):
    value = read(chunks[0])
    for i in range(1, len(chunks)):
        value = jnp.where(index == i, read(chunks[i]), value)
    return value


def attend_kernel(parts, aheads, count, with_text, resumed, final, info, *refs):
    queries, refs = refs[:parts], refs[parts:]
    keys, refs = list(refs[:count]), refs[count:]
    text = None
    if with_text:
        text, refs = refs[0], refs[1:]
    states, refs = refs[: 2 * len(aheads) * resumed], refs[2 * len(aheads) * resumed :]
    outs, (s_buf, m_buf, *o_buf) = refs[: len(aheads) * (2 - final)], refs[len(aheads) * (2 - final) :]
    heads, block = keys[0].shape[1], keys[0].shape[3]
    contract = (((0,), (0,)), ((), ()))

    def fold(s):
        return jnp.max(s.reshape(s.shape[0] // 8, 8, s.shape[1]), axis=0)

    group = s_buf.shape[1] // len(aheads)
    items = [(n, u) for n in range(len(aheads)) for u in range(group)]

    def score(stage, slot):
        for j, (n, u) in enumerate(items):
            head = stage * group + u
            index = lax.rem(place_of(HEADS) + aheads[n], parts)
            q = pick_chunk(queries, index, lambda chunk: chunk[0, head])
            top = None
            for i, chunk in enumerate(keys):
                s = lax.dot_general(
                    chunk[1, head], q, contract, preferred_element_type=jnp.float32
                )
                s_buf[slot, j, i * block : (i + 1) * block, :] = s
                top = fold(s) if top is None else jnp.maximum(top, fold(s))
            if with_text:
                t = lax.dot_general(
                    text[0, head], q, contract, preferred_element_type=jnp.float32
                )
                live = lax.broadcasted_iota(jnp.int32, t.shape, 0) < info[0]
                t = jnp.where(live, t, -jnp.inf)
                s_buf[slot, j, count * block :, :] = t
                top = jnp.maximum(top, fold(t))
            m_buf[slot, j] = top

    def mix(stage, slot):
        for j, (n, u) in enumerate(items):
            head = stage * group + u
            top = jnp.max(m_buf[slot, j], axis=0, keepdims=True)
            o = None
            if resumed:
                before = states[2 * n + 1][head, 0:1, :]
                top = jnp.maximum(top, before)
                o = states[2 * n][head] * jnp.exp2(before - top)
            for i in range(count + with_text):
                if i < count:
                    s, v = s_buf[slot, j, i * block : (i + 1) * block, :], keys[i][2, head]
                else:
                    s, v = s_buf[slot, j, count * block :, :], text[1, head]
                e = jnp.exp2(s - top).astype(jnp.bfloat16)
                term = jnp.dot(v, e, preferred_element_type=jnp.float32)
                o = term if o is None else o + term
            if final:
                rows = pl.ds(aligned(head * HEAD_DIM, 8), HEAD_DIM)
                o_buf[n][rows, :] = o[:HEAD_DIM] / o[HEAD_DIM : HEAD_DIM + 1]
            else:
                outs[2 * n][head] = o
                outs[2 * n + 1][head] = jnp.broadcast_to(top, (8, block))

    stages = heads // group
    score(0, 0)

    def step(i, carry):
        score(2 * i + 1, 1)
        mix(2 * i, 0)
        score(2 * i + 2, 0)
        mix(2 * i + 1, 1)
        return carry

    lax.fori_loop(0, stages // 2 - 1, step, 0)
    score(stages - 1, 1)
    mix(stages - 2, 0)
    mix(stages - 1, 1)
    if final:
        for n in range(len(aheads)):
            outs[n][...] = o_buf[n][...].astype(jnp.bfloat16)


def attend_call(info, queries, keys, text, states, aheads, final):
    parts, count = len(queries), len(keys)
    _, heads, _, block = keys[0].shape
    rows = block * count + (text.shape[3] if text is not None else 0)
    items = len(aheads) * (2 if count == 1 and heads % 4 == 0 else 1)
    if final:
        shapes = [((heads * HEAD_DIM, block), jnp.bfloat16)] * len(aheads)
        extra = [pltpu.VMEM((heads * HEAD_DIM, block), jnp.float32)] * len(aheads)
    else:
        shapes = [
            ((heads, HEAD_ROWS, block), jnp.float32),
            ((heads, 8, block), jnp.float32),
        ] * len(aheads)
        extra = []
    return resident(
        functools.partial(
            attend_kernel,
            parts,
            aheads,
            count,
            int(text is not None),
            int(bool(states)),
            int(final),
        ),
        shapes,
        info,
        list(queries) + list(keys) + ([text] if text is not None else []) + list(states),
        [
            pltpu.VMEM((2, items, rows, block), jnp.float32),
            pltpu.VMEM((2, items, 8, block), jnp.float32),
        ]
        + extra,
        4 * heads * 256 * block * rows * len(aheads),
        12,
        heads * block * rows * len(aheads),
    )


def out_kernel(n, extra, seq, blocks, share, info, *refs):
    att, refs = refs[:n], refs[n:]
    tokens, refs = refs[: n * len(blocks)], refs[n * len(blocks) :]
    w, refs = refs[: len(blocks)], refs[len(blocks) :]
    outs, (a, held) = refs[:-2], refs[-2:]
    width = att[0].shape[0]
    lanes = outs[0].shape[1]
    index = place_of(HEADS)
    skip = 0 if extra else width
    for r in range(n):
        a[pl.ds(aligned(base_of(n, r, width)), width), :] = att[r][...]
    far_w = [w[b][...] for b, key in enumerate(blocks) if key[0]]
    if far_w:
        far_y = jnp.dot(
            jnp.concatenate(far_w, axis=0), a[...], preferred_element_type=jnp.float32
        )
    done = 0
    for b, key in enumerate(blocks):
        count = w[b].shape[0]
        if key[0]:
            y = far_y[done : done + count]
            done += count
            offset = aligned(quarter_of(key, count, *share))
            inner, rows = pl.ds(offset, count), pl.ds(aligned(key[0] * width - skip + offset), count)
        else:
            y = jnp.dot(w[b][...], a[...], preferred_element_type=jnp.float32)
            inner, rows = slice(0, width), slice(0, width)
        x = pick_chunk(tokens[b * n : (b + 1) * n], index, lambda t: t[inner, :])
        held[rows, :] = (x.astype(jnp.float32) + y).astype(jnp.bfloat16)
    row = lax.broadcasted_iota(jnp.int32, (16, lanes), 0)
    numer, denom = info[1].astype(jnp.float32), info[2].astype(jnp.float32)
    tail = jnp.where(row == 0, numer, jnp.where(row == 1, denom, 0.0)).astype(jnp.bfloat16)
    outs = list(outs)
    for start, stop in [(0, width)] * bool(extra) + [(width, D)] * (held.shape[0] > width or not extra):
        for m in range(seq // 2):
            out = outs.pop(0)
            dest = lax.rem(lax.rem(place_of(SEQ), seq // 2) + m, seq // 2)
            span = pl.ds(aligned(dest * lanes, LANES), lanes)
            out[0 : stop - start, :] = held[start - skip : stop - skip, span]
            if start == 0:
                out[stop:, :] = tail


def out_call(info, att, tokens, w, extra, seq, blocks, share):
    n = len(att)
    width, count = att[0].shape
    total = sum(x.shape[0] for x in w)
    own = [((width + extra, 2 * count // seq), jnp.bfloat16)] * (seq // 2)
    other = [((D - width, 2 * count // seq), jnp.bfloat16)] * (seq // 2)
    return resident(
        functools.partial(out_kernel, n, extra, seq, blocks, share),
        own * bool(extra) + other * (total > width or not extra),
        info,
        list(att) + [x for group in tokens for x in group] + list(w),
        [pltpu.VMEM((D, count), jnp.bfloat16), pltpu.VMEM((total, count), jnp.bfloat16)],
        2 * D * total * count,
        12,
    )


def time_attend(read, att, rows, frames, heads):
    query, key, value = [
        [read(kind, f).reshape(heads, HEAD_DIM, read(kind, f).shape[1]) for f in range(frames)]
        for kind in range(3)
    ]
    lanes = query[0].shape[2]
    for f in range(frames):
        scores = [
            jnp.sum(query[f] * key[g], axis=1, keepdims=True) * HEAD_DIM ** (-0.5)
            for g in range(frames)
        ]
        top = functools.reduce(jnp.maximum, scores)
        expons = [jnp.exp(x - top) for x in scores]
        bottom = functools.reduce(jnp.add, expons)
        result = None
        for g in range(frames):
            weight = (expons[g] / bottom).astype(jnp.bfloat16).astype(jnp.float32)
            term = weight * value[g]
            result = term if result is None else result + term
        att[rows, f * lanes : (f + 1) * lanes] = result.reshape(
            heads * HEAD_DIM, lanes
        ).astype(jnp.bfloat16)


def time_project(near, far, gain, w, xs, inverse, out, parts, done=None):
    lanes = near[0].shape[1]
    width = w.shape[1]
    for f in range(len(near)):
        cols = slice(f * lanes, (f + 1) * lanes)
        total = None
        for r in range(parts):
            base = base_of(parts, r, width)
            if r == 0:
                x = near[f][0:width, :]
            else:
                x = far[f][(r - 1) * width : r * width, :]
            x = x.astype(jnp.float32)
            xs[pl.ds(aligned(base), width), cols] = (
                x * gain[pl.ds(aligned(D + base), width), :]
            ).astype(jnp.bfloat16)
            sq = jnp.sum(x * x, axis=0, keepdims=True)
            total = sq if total is None else total + sq
        inverse[:, cols] = jnp.broadcast_to(lax.rsqrt(total / D + epsilon), (8, lanes))
    for top in range(0, width, width // 2):
        span = slice(top, top + width // 2)
        for kind in range(3):
            y = jnp.dot(w[kind, span, :], xs[...], preferred_element_type=jnp.float32)
            out[kind, span, :] = (y * inverse[0:1, :]).astype(jnp.bfloat16)
        if done is not None:
            done(span)


def time_cross_kernel(frames, parts, info, *refs):
    near, far, refs = refs[:frames], refs[frames : 2 * frames], refs[2 * frames :]
    gain, w, xs, inverse, out = refs
    time_project(near, far, gain, w, xs, inverse, out, parts)


def time_near_kernel(frames, parts, share, info, *refs):
    near, far, refs = refs[:frames], refs[frames : 2 * frames], refs[2 * frames :]
    gain, w, crossed, xs, inverse, att, out = refs
    lanes = near[0].shape[1]
    rows = w.shape[1] // share

    def attend(part):
        for top in range(part.start, part.stop, rows):
            span = slice(top, top + rows)

            def read(kind, f):
                source = out if f < frames else crossed
                start = f % frames * lanes
                return source[kind, span, start : start + lanes].astype(jnp.float32)

            time_attend(read, att, span, 2 * frames, rows // HEAD_DIM)

    time_project(near, far, gain, w, xs, inverse, out, parts, attend)


def time_far_kernel(frames, share, keys, width, info, *refs):
    sides, refs = (refs[0:2], refs[2:4]), refs[4:]
    w, att = refs[:-1], refs[-1]
    rows = w[0].shape[0]
    half = frames // 2
    lanes = att.shape[1] // frames
    for b, key in enumerate(keys):
        span = pl.ds(aligned((key[0] - 1) * width + quarter_of(key, rows, *share)), rows)
        made = []
        for kind in range(3):
            part = w[2 * b][...] if kind == 0 else w[2 * b + 1][(kind - 1) * rows : kind * rows, :]
            for xs, inverse in sides:
                y = jnp.dot(part, xs[...], preferred_element_type=jnp.float32)
                made.append((y * inverse[0:1, :]).astype(jnp.bfloat16).astype(jnp.float32))

        def read(kind, f):
            start = f % half * lanes
            return made[2 * kind + f // half][:, start : start + lanes]

        time_attend(read, att, span, frames, rows // HEAD_DIM)


def time_cross_call(info, near, far, gain, w, parts):
    frames, lanes = len(near), near[0].shape[1]
    width, count = w.shape[1], frames * lanes
    return resident(
        functools.partial(time_cross_kernel, frames, parts),
        [
            ((D, count), jnp.bfloat16),
            ((8, count), jnp.float32),
            ((3, width, count), jnp.bfloat16),
        ],
        info,
        list(near) + list(far) + [gain, w],
        [],
        6 * D * width * count,
        12,
    )


def time_near_call(info, near, far, gain, w, crossed, parts, share):
    frames, lanes = len(near), near[0].shape[1]
    width, count = w.shape[1], frames * lanes
    return resident(
        functools.partial(time_near_kernel, frames, parts, share),
        [
            ((D, count), jnp.bfloat16),
            ((8, count), jnp.float32),
            ((width, 2 * count), jnp.bfloat16),
        ],
        info,
        list(near) + list(far) + [gain, w, crossed],
        [pltpu.VMEM((3, width, count), jnp.bfloat16)],
        6 * D * width * count,
        12,
    )


def time_far_call(info, sides, w, frames, share, keys, width):
    count = 2 * sides[0].shape[1]
    return resident(
        functools.partial(time_far_kernel, frames, share, keys, width),
        [((D - width, count), jnp.bfloat16)],
        info,
        list(sides) + list(w),
        [],
        6 * D * (D - width) * count,
        12,
    )[0]


def time_out_kernel(frames, parts, share, keys, first, own, info, *refs):
    near, refs = refs[:frames], refs[frames:]
    far, refs = refs[:frames], refs[frames:]
    att_near, att_far, refs = refs[0], refs[1], refs[2:]
    o_own, refs = (refs[0], refs[1:]) if own else (None, refs)
    o_far, (keep, send, ratios, att, res) = refs[: len(keys)], refs[len(keys) :]
    lanes = near[0].shape[1]
    width = att_near.shape[0]
    head_index, branch = place_of(HEADS), place_of(CFG)
    cols = slice(first * lanes, (first + frames) * lanes)
    for r in range(parts):
        span = pl.ds(aligned(base_of(parts, r, width)), width)
        att[span, :] = (
            att_near[:, cols] if r == 0 else att_far[(r - 1) * width : r * width, cols]
        )

    def add(y, source, start, rows):
        for f in range(frames):
            x = source[f][start, :].astype(jnp.float32) + y[:, f * lanes : (f + 1) * lanes]
            res[f, rows, :] = x.astype(jnp.bfloat16)

    if own:
        y = jnp.dot(o_own[...], att[...], preferred_element_type=jnp.float32)
        add(y, near, slice(0, width), pl.ds(aligned(base_of(parts, 0, width)), width))
    if keys:
        far_y = jnp.dot(
            jnp.concatenate([x[...] for x in o_far], axis=0),
            att[...],
            preferred_element_type=jnp.float32,
        )
    done = 0
    for i, key in enumerate(keys):
        count = o_far[i].shape[0]
        offset = quarter_of(key, count, *share)
        add(
            far_y[done : done + count],
            far,
            pl.ds(aligned((key[0] - 1) * width + offset), count),
            pl.ds(aligned(base_of(parts, key[0], width) + offset), count),
        )
        done += count
    slot = keep.shape[2]
    for f in range(frames):
        tail = near[f][width:, :].astype(jnp.float32)
        ratios[f : f + 1, :] = tail[0:1] / tail[1:2]
        for n in range(keep.shape[1]):
            head = lax.rem(head_index + n + (0 if own else 1), parts)
            keep[f, n] = res[f, pl.ds(aligned((head * 2 + branch) * slot), slot), :]
            send[f, n] = res[f, pl.ds(aligned((head * 2 + 1 - branch) * slot), slot), :]


def time_out_call(info, near, far, att_near, att_far, o_own, o_far, parts, share, keys, first):
    frames, lanes = len(near), near[0].shape[1]
    own = [] if o_own is None else [o_own]
    count = len(own) + (parts - 1 if keys else 0)
    result = ((frames, count, D // (2 * parts), lanes), jnp.bfloat16)
    return resident(
        functools.partial(time_out_kernel, frames, parts, share, keys, first, bool(own)),
        [result, result, ((frames, lanes), jnp.float32)],
        info,
        list(near) + list(far) + [att_near, att_far] + own + list(o_far),
        [
            pltpu.VMEM((D, frames * lanes), jnp.bfloat16),
            pltpu.VMEM((frames, D, lanes), jnp.bfloat16),
        ],
        2 * D * D * frames * lanes * count // parts,
        12,
    )


def guide_kernel(info, keep, other, ratios, *outs):
    frames, parts = keep.shape[0], keep.shape[1]
    branch = place_of(CFG)
    for f in range(frames):
        ratio = ratios[f : f + 1, :]
        for r in range(parts):
            mine = keep[f, r].astype(jnp.float32)
            theirs = other[f, r].astype(jnp.float32)
            cond = jnp.where(branch == 0, mine, theirs)
            uncond = jnp.where(branch == 0, theirs, mine)
            outs[f * parts + r][...] = (uncond + ratio * (cond - uncond)).astype(jnp.bfloat16)


def place_kernel(seq, parts, *refs):
    pieces, out, sems = refs[:-2], refs[-2], refs[-1]
    head, frame = place_of(HEADS), place_of(SEQ)
    half = seq // 2
    copies = []
    for i, (cross, m) in enumerate(roads(seq)):
        side = crossing(seq, cross) * half + lax.rem(lax.rem(frame, half) + m, half)
        for r in range(parts):
            piece = pieces[i * parts + r]
            slot = lax.rem(head - r + parts, parts) * seq + side
            lanes = piece.shape[1]
            view = out.at[:, pl.ds(aligned(slot * lanes, LANES), lanes)]
            copies.append(pltpu.make_async_copy(piece, view, sems.at[i * parts + r]))
    for copy in copies:
        copy.start()
    for copy in copies:
        copy.wait()


def place_call(pieces, seq, parts):
    rows, lanes = pieces[0].shape
    n = len(pieces)
    return pl.pallas_call(
        functools.partial(place_kernel, seq, parts),
        out_shape=jax.ShapeDtypeStruct((rows, n * lanes), jnp.bfloat16),
        in_specs=[pl.BlockSpec(memory_space=pltpu.VMEM)] * n,
        out_specs=pl.BlockSpec(memory_space=pltpu.HBM),
        scratch_shapes=[pltpu.SemaphoreType.DMA((n,))],
        compiler_params=pltpu.CompilerParams(vmem_limit_bytes=4 << 20),
    )(*[local(x) for x in pieces])


def split_kernel(seq, parts, source, *refs):
    outs, sems = refs[:-1], refs[-1]
    copies = []
    for i, out in enumerate(outs):
        block = out.shape[1]
        start = ((i % parts) * 2 + crossing(seq, i < parts)) * block
        view = source.at[:, pl.ds(aligned(start, LANES), block)]
        copies.append(pltpu.make_async_copy(view, out, sems.at[i]))
    for copy in copies:
        copy.start()
    for copy in copies:
        copy.wait()


def pick_kernel(share, w_out, w_time, w_last, w_space, gains, *refs):
    outs, w_here, column, sems = refs[:-3], refs[-3], refs[-2], refs[-1]
    rows = outs[-1].shape[0]
    start = quarter_of((0, 0, 0), rows, *share)
    inner = start + lax.rem(place_of(SEQ), 2) * outs[0].shape[0]
    moves = [
        (w_out, inner, outs[0]),
        (w_time.at[0], inner, outs[1]),
        (w_time.at[1], start, outs[2].at[0:rows, :]),
        (w_time.at[2], start, outs[2].at[rows:, :]),
        (w_last, start, outs[3]),
        (w_space, None, w_here),
    ]
    copies = []
    for i, (source, first, out) in enumerate(moves):
        view = source if first is None else source.at[pl.ds(aligned(first, 8), out.shape[0]), :]
        copies.append(pltpu.make_async_copy(view, out, sems.at[i]))
    for copy in copies:
        copy.start()
    row = lax.broadcasted_iota(jnp.int32, (LANES, LANES), 0)
    diagonal = row == lax.broadcasted_iota(jnp.int32, (LANES, LANES), 1)
    for i in range(gains.shape[0]):
        wide = jnp.broadcast_to(gains[i : i + 1, :].astype(jnp.float32), (LANES, LANES))
        column[i * LANES : (i + 1) * LANES, :] = jnp.sum(
            jnp.where(diagonal, wide, 0.0), axis=1, keepdims=True
        )
    for copy in copies:
        copy.wait()


def stack_kernel(own, other, out, sems):
    rows = own.shape[0]
    side = lax.rem(place_of(SEQ), 2)
    copies = [
        pltpu.make_async_copy(own, out.at[pl.ds(aligned(side * rows, 8), rows), :], sems.at[0]),
        pltpu.make_async_copy(
            other, out.at[pl.ds(aligned((1 - side) * rows, 8), rows), :], sems.at[1]
        ),
    ]
    for copy in copies:
        copy.start()
    for copy in copies:
        copy.wait()


def stack_call(own, other):
    rows, columns = own.shape
    place = pl.BlockSpec(memory_space=pltpu.VMEM)
    return pl.pallas_call(
        stack_kernel,
        out_shape=pltpu.VMEM((2 * rows, columns), own.dtype),
        in_specs=[place, place],
        out_specs=place,
        scratch_shapes=[pltpu.SemaphoreType.DMA((2,))],
        compiler_params=pltpu.CompilerParams(vmem_limit_bytes=2 << 20),
    )(local(own), local(other))


def roads(seq):
    return [(cross, m) for cross in (0, 1) for m in range(seq // 2)]


def follow(seq, road, i, back=False):
    cross, m = road
    half = seq // 2
    side = i // half
    return (1 - side if cross else side) * half + (i % half + (-m if back else m)) % half


def shift(x, axis, by):
    size = lax.axis_size(axis)
    return lax.ppermute(x, axis, [(i, (i + by) % size) for i in range(size)])


def after(x, *gates):
    return lax.optimization_barrier((x,) + gates)[0]


def shards(fit, *args):
    (video_tokens, _, _, _, _, _, _, _, _, _, _) = args
    heads, seq = lax.axis_size(HEADS), lax.axis_size(SEQ)
    positions = video_tokens.shape[3]
    lanes = positions // (heads * seq)
    if not fit or lanes % LANES or seq % 4 or video_tokens.shape[1] != 1:
        return shards_plain(*args)
    return shards_fast(*args)


def shards_fast(
    video_tokens,
    text_tokens,
    text_length,
    guide_numer,
    guide_denom,
    spatial_gain,
    spatial_qkv,
    spatial_out,
    temporal_gain,
    temporal_qkv,
    temporal_out,
):
    heads, seq = lax.axis_size(HEADS), lax.axis_size(SEQ)
    groups, cfg = lax.axis_size(GROUPS), lax.axis_size(CFG)
    positions = video_tokens.shape[3]
    lanes = positions // (heads * seq)
    video, text = video_tokens[0, 0], text_tokens[0, 0]
    width = video.shape[0]
    rows = width // (groups * cfg)
    per = 2
    block = positions // (heads * per)
    ring = range(1, heads)
    info = jnp.concatenate([text_length[0], guide_numer, guide_denom])
    gains = jnp.concatenate([spatial_gain, temporal_gain]).reshape(-1, LANES)

    text_set = [text] + [shift(text, HEADS, r) for r in ring]
    parts = pl.pallas_call(
        functools.partial(split_kernel, seq, heads),
        out_shape=(jax.ShapeDtypeStruct((width, block), jnp.bfloat16),) * (heads * per),
        in_specs=[pl.BlockSpec(memory_space=pltpu.HBM)],
        out_specs=(pl.BlockSpec(memory_space=pltpu.VMEM),) * (heads * per),
        scratch_shapes=[pltpu.SemaphoreType.DMA((heads * per,))],
        compiler_params=pltpu.CompilerParams(vmem_limit_bytes=8 << 20),
    )(pltpu.with_memory_space_constraint(video, pltpu.HBM))
    chunk_sets = []
    for part in parts:
        chunk_sets.append([part] + [shift(part, HEADS, r) for r in ring])

    sources = [
        pltpu.with_memory_space_constraint(x, pltpu.HBM)
        for x in (spatial_out, temporal_qkv, temporal_out, spatial_qkv)
    ]
    whole, part = (rows, D), (rows // 2, D)
    *mine, spatial_here, gain = pl.pallas_call(
        functools.partial(pick_kernel, (groups, cfg)),
        out_shape=tuple(
            jax.ShapeDtypeStruct(shape, jnp.bfloat16)
            for shape in (part, part, (2 * rows, D), whole)
        )
        + (
            pltpu.VMEM(spatial_qkv.shape, jnp.bfloat16),
            pltpu.VMEM((2 * D, 1), jnp.float32),
        ),
        in_specs=[pl.BlockSpec(memory_space=pltpu.HBM)] * 4
        + [pl.BlockSpec(memory_space=pltpu.VMEM)],
        out_specs=(pl.BlockSpec(memory_space=pltpu.VMEM),) * 6,
        scratch_shapes=[pltpu.SemaphoreType.DMA((6,))],
        compiler_params=pltpu.CompilerParams(vmem_limit_bytes=12 << 20),
    )(*sources, gains)

    chunks = []
    mark, states = None, []
    aheads = list(range(1, heads)) + [0]
    for j, chunk in enumerate(chunk_sets):
        if j == 0:
            text_kv, made = project_call(
                info, [text_set, chunk], [(1, 2), (0, 1, 2)], gain, spatial_here
            )
        else:
            ready = [chunk[0]] + [after(x, mark) for x in chunk[1:]]
            (made,) = project_call(info, [ready], [(0, 1, 2)], gain, spatial_here)
        chunks.append(made)
        mark = made
        if heads - 1 <= j < heads * per - 1:
            fresh = chunks if j == heads - 1 else [made]
            states = attend_call(
                info,
                chunks[:heads],
                fresh,
                text_kv if j == heads - 1 else None,
                states,
                aheads,
                False,
            )
            mark = states[0]

    keys = [(r, dg, dc) for r in ring for dg in range(groups) for dc in range(cfg)]

    def first_hop(w, gate=None):
        w = w if gate is None else after(w, gate)
        return {(r, 0, 0): shift(w, HEADS, r) for r in ring}

    def trade(held, gate):
        pairs = [(i, i ^ 1) for i in range(seq)]
        for r in ring:
            own = after(held[r, 0, 0], gate)
            held[r, 0, 0] = own, lax.ppermute(own, SEQ, pairs)

    def join(held, gate):
        for r in ring:
            own, other = held[r, 0, 0]
            held[r, 0, 0] = stack_call(own, after(other, gate))

    def second_hop(held, gate):
        for r in ring:
            for dg in range(1, groups):
                source = after(held[r, 0, 0], gate)
                held[r, dg, 0] = shift(source, GROUPS, dg)

    def third_hop(held, gate):
        for r in ring:
            for dg in range(groups):
                for dc in range(1, cfg):
                    source = after(held[r, dg, 0], gate)
                    held[r, dg, dc] = shift(source, CFG, dc)

    far_out = first_hop(mine[0])
    far_time = [first_hop(mine[1])]
    att = {}

    def attend(cross, r):
        if cross:
            n = aheads.index(r)
            state = states[2 * n : 2 * n + 2]
            return attend_call(info, chunks[:heads], chunks[-1:], None, state, [r], True)[0]
        return attend_call(info, chunks[heads:], chunks, text_kv, [], [r], True)[0]

    def attend_far(cross):
        for r in ring:
            mark = attend(cross, r)
            att[cross, r] = shift(mark, HEADS, r)
        return mark

    def held_tokens(r, cross):
        return [x[r] for x in (chunk_sets[:heads] if cross else chunk_sets[heads:])]

    split = (groups, cfg)
    near, far = {}, {}

    def out_rows(cross, own, others):
        att_all = [att[cross, r] for r in range(heads)]
        part = [(0, 0, 0)] * own + keys * others
        got = out_call(
            info,
            att_all,
            [held_tokens(key[0], cross) for key in part],
            [far_out[key] if key[0] else spatial_out for key in part],
            16 * own,
            seq,
            part,
            split,
        )
        if own:
            near.update({(cross, m): got[m] for m in range(seq // 2)})
        if others:
            far.update({(cross, m): got[m + seq // 2 * own] for m in range(seq // 2)})
        return got[0]

    first = attend_far(1)
    trade(far_out, first)
    att[1, 0] = attend(1, 0)
    trade(far_time[0], att[1, 0])
    join(far_out, att[1, 0])
    second_hop(far_out, att[1, 0])
    early = out_rows(1, 1, 0)
    join(far_time[0], early)
    third_hop(far_out, early)
    second = attend_far(0)
    middle = out_rows(1, 0, 1)
    att[0, 0] = attend(0, 0)
    late = out_rows(0, 1, 1)
    far_time.append(first_hop(mine[2], first))
    far_last = first_hop(mine[3], second)
    for name, held, gate in zip("qk", far_time, (early, middle)):
        second_hop(held, gate)
        third_hop(held, late)

    def send_all(held):
        moved = []
        for road in roads(seq):
            x = held[road]
            if road != (0, 0):
                route = [(i, follow(seq, road, i)) for i in range(seq)]
                x = lax.ppermute(x, SEQ, route)
            moved.append(x)
        return moved

    near, far = send_all(near), send_all(far)
    second_hop(far_last, far[seq // 2])
    third_hop(far_last, far[seq // 2])
    share = groups * cfg
    mid = seq // 2
    xs_cross, inverse_cross, crossed = time_cross_call(
        info, near[mid:], far[mid:], gain, temporal_qkv, heads
    )
    xs, inverse, att_near = time_near_call(
        info, near[:mid], far[:mid], gain, temporal_qkv, crossed, heads, share
    )
    att_far = time_far_call(
        info,
        [xs, inverse, xs_cross, inverse_cross],
        [far_time[kind][key] for key in keys for kind in range(2)],
        seq,
        split,
        keys,
        width,
    )
    slot = D // (heads * cfg)
    landed = {}
    results = {}
    jobs = [(1, 1, 0), (1, 0, 1), (0, 1, 1)]
    for cross, own, others in jobs:
        name = f"{cross}{own}"
        picked = [i for i, road in enumerate(roads(seq)) if road[0] == cross]
        part = keys * others
        keep, send, ratios = time_out_call(
            info,
            [near[i] for i in picked],
            [far[i] for i in picked],
            att_near,
            att_far,
            temporal_out if own else None,
            [far_last[key] for key in part],
            heads,
            split,
            part,
            picked[0],
        )
        results[name] = keep, shift(send, CFG, 1), ratios
    for cross, own, others in jobs:
        name = f"{cross}{own}"
        picked = [i for i, road in enumerate(roads(seq)) if road[0] == cross]
        sides = list(range(1 - own, 1 + (heads - 1) * others))
        pieces = resident(
            guide_kernel,
            [((slot, lanes), jnp.bfloat16)] * (len(picked) * len(sides)),
            info,
            results[name],
            [],
            len(picked) * D * lanes,
            8,
        )
        for n, i in enumerate(picked):
            road = roads(seq)[i]
            for k, r in enumerate(sides):
                piece = pieces[n * len(sides) + k]
                if road != (0, 0) or r:
                    route = [
                        (a * heads + b, follow(seq, road, a, True) * heads + (b + r) % heads)
                        for a in range(seq)
                        for b in range(heads)
                    ]
                    piece = lax.ppermute(piece, (SEQ, HEADS), route)
                landed[i, r] = piece
    landed = [landed[i, r] for i in range(seq) for r in range(heads)]
    result = place_call(landed, seq, heads)
    return result[None]


def solution(mesh):
    return jax.shard_map(
        functools.partial(shards, fits(mesh)),
        mesh=mesh,
        in_specs=(
            P(CFG, (GROUPS, SEQ), HEADS, None),
            P(CFG, (GROUPS, SEQ), HEADS, None),
            P(CFG, (GROUPS, SEQ)),
            P((GROUPS, SEQ)),
            P((GROUPS, SEQ)),
            P(),
            P(None, HEADS, None),
            P(HEADS, None),
            P(),
            P(None, HEADS, None),
            P(HEADS, None),
        ),
        out_specs=P((GROUPS, SEQ), (HEADS, CFG), None),
        check_vma=False,
    )
```
